32 devices in a mesh: clips: 2 (over y), space: 4 (over z), tm: 2 (over x), chan: 2 (over core).
Axes of the slice: x: 2, y: 2, z: 4, core: 2. Of those that a mesh axis runs over, the one named last changes fastest.
Arguments:
- frames_in: bfloat16 [4, 16, 160, 384], P(('clips', 'tm'), 'space', None, 'chan'), parts along dimension 0, may hold values from -6 to 6
- cache: bfloat16 [4, 16, 160, 384], P('clips', 'space'), parts along dimension 0, may hold values from -6 to 6
- gain_one: bfloat16 [384], replicated, may hold values from 0.099609375 to 1.8984375
- gain_two: bfloat16 [384], replicated, may hold values from 0.099609375 to 1.8984375
- w_query: bfloat16 [384, 384], replicated, may hold values from -10 to 10
- w_key: bfloat16 [384, 384], replicated, may hold values from -10 to 10
- w_value: bfloat16 [384, 384], replicated, may hold values from -0.3125 to 0.3125
- w_out: bfloat16 [384, 384], replicated, may hold values from -0.3125 to 0.3125
- conv_weight: bfloat16 [3, 3, 3, 384, 384], P(None, None, None, None, 'chan'), may hold values from -0.0625 to 0.0625
Outputs:
- decoded: bfloat16 [4, 16, 160, 384], P(('clips', 'tm'), 'space', None, 'chan'), parts along dimension 0
The draws below stay inside these ranges and needn't reach their ends.
There are 2 independent parts, one for each index of `clips`. The reference program is written for one: setup_inputs(seed, part) draws one part's arguments, and reference() takes and returns one part's arrays. A program takes and returns all parts, laid end to end along the dimension named above; an argument that names none is the same for every part. Nothing has to cross between parts.
All inputs are finite; a program needn't handle non-finite values.
Results may differ from the reference program's by a relative error of at most 0.0062.
Values may be sent and summed in bfloat16 or wider, within the bound.
A program may use at most 128 MiB of HBM per device.

```python
import math
import jax
import jax.numpy as jnp
from jax import lax

C = 384
W = 160
F = 2
H = 16


def projection_draw(key, salt):
    scatter = jax.random.truncated_normal(jax.random.fold_in(key, salt), -4.0, 4.0, (C, C), jnp.float32) / math.sqrt(C)
    return (1.75 * scatter).astype(jnp.bfloat16)


def draw_w_query(key, part):
    return projection_draw(key, 11)


def draw_w_key(key, part):
    return projection_draw(key, 13)


def draw_frames_in(key, part):
    return jax.random.truncated_normal(jax.random.fold_in(key, 25), -6.0, 6.0, (F, H, W, C), jnp.float32).astype(jnp.bfloat16)


def steps_of(stream_key, shape, pieces, smallest, high):
    level, own = 1.0, jax.random.fold_in(stream_key, 6)
    for dim, shards_of in pieces:
        draws = jnp.exp(jax.random.uniform(jax.random.fold_in(own, dim), (shards_of,), jnp.float32, smallest / len(pieces), high / len(pieces)))
        level = level * jnp.repeat(draws, shape[dim] // shards_of).reshape([-1 if axis == dim else 1 for axis in range(len(shape))])
    return level


def scatter_about(stream_key, extent, spread, most, cuts=(), held_as=jnp.bfloat16):
    entries = jax.random.normal(stream_key, extent, jnp.float32) * spread
    if len(cuts) > 0:
        entries = steps_of(stream_key, extent, cuts, -0.22, 0.18) * entries
    return jnp.clip(entries, min=-most, max=most).astype(held_as)


def setup_inputs(seed: int = 0, part: int = 0) -> dict:
    key_of = jax.random.split(jax.random.key(seed), 10)
    own_keys = jax.random.split(jax.random.fold_in(key_of[9], part), 10)
    frames_in = draw_frames_in(jax.random.fold_in(jax.random.fold_in(key_of[9], part), 71), part)
    cache = scatter_about(own_keys[1], (2, H, W, C), 1.0, 6.0, ((1, 4),))
    gain_one = jnp.clip(1.0 + 0.18 * jax.random.normal(key_of[2], (C,), jnp.float32), 0.099609375, 1.8984375).astype(jnp.bfloat16)
    gain_two = jnp.clip(1.0 + 0.18 * jax.random.normal(key_of[3], (C,), jnp.float32), 0.099609375, 1.8984375).astype(jnp.bfloat16)
    w_query = draw_w_query(jax.random.fold_in(key_of[9], 71), part)
    w_key = draw_w_key(jax.random.fold_in(key_of[9], 71), part)
    w_value = scatter_about(key_of[6], (C, C), C ** -0.5, 0.3125)
    w_out = scatter_about(key_of[7], (C, C), C ** -0.5, 0.3125)
    conv_weight = scatter_about(key_of[8], (3, 3, 3, C, C), (27 * C) ** -0.5, 0.0625, ((4, 2),))
    return dict(frames_in=frames_in, cache=cache, gain_one=gain_one, gain_two=gain_two, w_query=w_query, w_key=w_key, w_value=w_value, w_out=w_out, conv_weight=conv_weight)


def rms_scaled(values, gain):
    wide = values.astype(jnp.float32)
    factor = lax.rsqrt(lax.optimization_barrier(jnp.mean(wide * wide, axis=-1, keepdims=True)) + 1e-06)
    return wide * factor * gain.astype(jnp.float32)

def frame_attention(frame, gain_one, w_query, w_key, w_value, w_out):
    tokens = frame.reshape(-1, C)
    normed = rms_scaled(tokens, gain_one).astype(jnp.bfloat16)
    query = jnp.dot(normed, w_query, preferred_element_type=jnp.float32).astype(jnp.bfloat16)
    keys = jnp.dot(normed, w_key, preferred_element_type=jnp.float32).astype(jnp.bfloat16)
    values = jnp.dot(normed, w_value, preferred_element_type=jnp.float32).astype(jnp.bfloat16)
    block = math.gcd(tokens.shape[0], 512)
    blocks = query.reshape(-1, block, C)

    def one_block(rows):
        scores = jnp.einsum('qc,kc->qk', rows.astype(jnp.float32), keys.astype(jnp.float32)) * C ** (-0.5)
        top = lax.optimization_barrier(jnp.max(scores, axis=-1, keepdims=True))
        weights = jnp.exp(scores - top)
        total = lax.optimization_barrier(jnp.sum(weights, axis=-1, keepdims=True))
        mixed = jnp.dot(weights.astype(jnp.bfloat16), values, preferred_element_type=jnp.float32) / total
        return mixed.astype(jnp.bfloat16)
    attended = lax.map(one_block, blocks).reshape(-1, C)
    joined = tokens.astype(jnp.float32) + jnp.dot(attended, w_out, preferred_element_type=jnp.float32)
    return joined.astype(jnp.bfloat16).reshape(frame.shape)

def reference(frames_in, cache, gain_one, gain_two, w_query, w_key, w_value, w_out, conv_weight):
    joined = lax.map(lambda frame: frame_attention(frame, gain_one, w_query, w_key, w_value, w_out), frames_in)
    act = jax.nn.silu(rms_scaled(joined, gain_two)).astype(jnp.bfloat16)
    extended = jnp.concatenate([cache, act], axis=0).astype(jnp.float32)
    extended = jnp.pad(extended, ((0, 0), (1, 1), (1, 1), (0, 0)))
    conv = lax.conv_general_dilated(extended[None], conv_weight.astype(jnp.float32), (1, 1, 1), 'VALID', dimension_numbers=('NDHWC', 'DHWIO', 'NDHWC'), precision=lax.Precision.HIGHEST)[0]
    return (joined.astype(jnp.float32) + conv).astype(jnp.bfloat16)
```

```python
import functools
import math

import jax
import jax.numpy as jnp
from jax import lax
from jax.experimental import pallas as pl
from jax.experimental.pallas import tpu as pltpu
from jax.sharding import PartitionSpec as P

F32 = jnp.float32
BF16 = jnp.bfloat16
MESH = pl.DeviceIdType.MESH


def normalized(wide, gain):
    factor = lax.rsqrt(jnp.mean(wide * wide, axis=-1, keepdims=True) + 1e-06)
    return wide * factor * gain.astype(F32)


def kernel(
    Z, N,
    x_hbm, cache_hbm, g1_ref, g2_ref, wq_hbm, wk_hbm, wv_hbm, wo_hbm, cw_hbm,
    out_ref,
    xr, xg, qk, top, total, acc, cb, jt, jo, parts, wq, wk, wv, wo, cw,
    s_loc, s_pair, r_pair, s_right, s_left, s_sib, r_z, r_sib,
    s_cache, r_halo, s_edge, s_rest, r_edge, r_rest, s_tm, r_tm,
):
    z = lax.axis_index("space")
    c = lax.axis_index("chan")
    tm = lax.axis_index("tm")
    o = 1 - c
    R, W, S = out_ref.shape[1:]
    C = 2 * S
    hr = R // 2
    half = hr * W
    T = R * W

    def dev(dz=None, core=None, frame=None):
        return {
            "space": z if dz is None else dz,
            "chan": c if core is None else core,
            "tm": tm if frame is None else frame,
        }

    def send(src, dst, ssem, rsem, to):
        return pltpu.make_async_remote_copy(
            src_ref=src, dst_ref=dst, send_sem=ssem, recv_sem=rsem,
            device_id=to, device_id_type=MESH,
        )

    near = z + 2 * c - 1
    has_near = jnp.logical_and(near >= 0, near < Z)

    barrier = pltpu.get_barrier_semaphore()

    def greet(to):
        pl.semaphore_signal(barrier, inc=1, device_id=to, device_id_type=MESH)

    greet(dev(core=o))
    pl.when(z > 0)(lambda: greet(dev(dz=z - 1)))
    pl.when(z < Z - 1)(lambda: greet(dev(dz=z + 1)))
    pl.when(has_near)(lambda: greet(dev(dz=near, core=o)))
    for hop in (1, 2):
        if N > hop:
            pl.when(tm >= hop)(functools.partial(lambda h: greet(dev(frame=tm - h)), hop))

    x_own = pltpu.make_async_copy(x_hbm.at[0, pl.ds(c * hr, hr)], xr.at[c], s_loc.at[0])
    x_own.start()
    weights = [
        pltpu.make_async_copy(a, b, s_loc.at[1 + i])
        for i, (a, b) in enumerate(((wq_hbm, wq), (wk_hbm, wk), (wv_hbm, wv), (wo_hbm, wo), (cw_hbm, cw)))
    ]
    for w in weights:
        w.start()
    first = jnp.minimum(tm, 1)
    cache_two = pltpu.make_async_copy(cache_hbm.at[first], cb.at[0, pl.ds(1, R)], s_loc.at[6])
    cache_one = pltpu.make_async_copy(cache_hbm.at[1], cb.at[1, pl.ds(1, R)], s_loc.at[7])
    pl.when(tm <= 1)(cache_two.start)
    pl.when(tm == 0)(cache_one.start)

    want = 1 + jnp.where(z > 0, 1, 0) + jnp.where(z < Z - 1, 1, 0) + jnp.where(has_near, 1, 0)
    for hop in (1, 2):
        if N > hop:
            want = want + jnp.where(tm + hop < N, 1, 0)
    pl.semaphore_wait(barrier, want)

    pair = send(x_hbm.at[0, pl.ds(o * hr, hr)], xr.at[c], s_pair.at[0], r_pair.at[0], dev(core=o))
    pair.start()

    blank = jnp.zeros((W, C), BF16)

    @pl.when(z == 0)
    def _():
        for f in range(3):
            cb[f, 0] = blank

    @pl.when(z == Z - 1)
    def _():
        for f in range(3):
            cb[f, R + 1] = blank

    x_own.wait()
    pair.wait_recv()

    def tokens():
        return jnp.concatenate(
            [xr[0].reshape(half, S).astype(F32), xr[1].reshape(half, S).astype(F32)], axis=-1
        )

    normed = normalized(tokens(), g1_ref[...]).astype(BF16)
    xg[z, c] = normed

    def rightward(j):
        return send(xg.at[j, c], xg.at[j, c], s_right.at[j], r_z.at[j], dev(dz=z + 1))

    def leftward(j):
        return send(xg.at[j, c], xg.at[j, c], s_left.at[j], r_z.at[j], dev(dz=z - 1))

    def sideward(j):
        return send(xg.at[j, c], xg.at[j, c], s_sib.at[j], r_sib.at[j], dev(core=o))

    pl.when(z < Z - 1)(rightward(z).start)
    pl.when(z > 0)(leftward(z).start)
    sideward(z).start()

    for w in weights[:2]:
        w.wait()
    query = jnp.dot(normed, wq[...], preferred_element_type=F32).astype(BF16)
    folded = lax.dot_general(query, wk[...], (((1,), (1,)), ((), ())), preferred_element_type=F32)
    qk[...] = (folded * (C ** (-0.5) * math.log2(math.e))).astype(BF16)
    top[...] = jnp.full(top.shape, -1e30, F32)
    total[...] = jnp.zeros(total.shape, F32)
    acc[...] = jnp.zeros(acc.shape, F32)

    def attend(j):
        keys = xg[j].reshape(T, C)
        scores = lax.dot_general(qk[...], keys, (((1,), (1,)), ((), ())), preferred_element_type=F32)
        old = top[...]
        new = jnp.maximum(old, jnp.max(scores, axis=-1, keepdims=True))
        weight = jnp.exp2(scores - new)
        fade = jnp.exp2(old - new)
        top[...] = new
        total[...] = total[...] * fade + jnp.sum(weight, axis=-1, keepdims=True)
        acc[...] = acc[...] * fade + jnp.dot(weight.astype(BF16), keys, preferred_element_type=F32)

    sideward(z).wait_recv()
    attend(z)

    def cache_edge(f, side):
        row = R - 1 if side == 0 else 0
        source = cache_hbm.at[first if f == 0 else 1, row]
        to = dev(dz=z + 1) if side == 0 else dev(dz=z - 1)
        return send(source, cb.at[f, 0 if side == 0 else R + 1], s_cache.at[f, side], r_halo.at[f, side], to)

    def cache_edges(act):
        for side, there in ((0, z < Z - 1), (1, z > 0)):
            pl.when(jnp.logical_and(there, tm <= 1))(lambda s=side: act(cache_edge(0, s)))
            pl.when(jnp.logical_and(there, tm == 0))(lambda s=side: act(cache_edge(1, s)))

    def step(d, carry):
        lo, hi = z - d, z + d
        has_lo, has_hi = lo >= 0, hi < Z

        @pl.when(has_lo)
        def _():
            rightward(lo).wait_recv()
            pl.when(z < Z - 1)(rightward(lo).start)
            sideward(lo).start()

        @pl.when(has_hi)
        def _():
            leftward(hi).wait_recv()
            pl.when(z > 0)(leftward(hi).start)
            sideward(hi).start()

        pl.when(d == Z - 1)(lambda: cache_edges(lambda copy: copy.start()))

        @pl.when(has_lo)
        def _():
            sideward(lo).wait_recv()
            attend(lo)

        @pl.when(has_hi)
        def _():
            sideward(hi).wait_recv()
            attend(hi)

        return carry

    lax.fori_loop(1, Z, step, 0)

    for w in weights[2:4]:
        w.wait()
    mixed = (acc[...] * (1.0 / total[...])).astype(BF16)
    attended = jnp.dot(mixed, wv[...], preferred_element_type=F32).astype(BF16)
    joined = tokens() + jnp.dot(attended, wo[...], preferred_element_type=F32)
    joined = joined.astype(BF16).astype(F32)
    scaled = normalized(joined, g2_ref[...])
    act = (scaled / (1.0 + jnp.exp(-scaled))).astype(BF16)
    mine = 1 + c * hr
    cb[2, pl.ds(mine, hr)] = act.reshape(hr, W, C)

    edge = jnp.where(c == 0, 1, R)
    rest = jnp.where(c == 0, 2, 1 + hr)
    far = jnp.where(c == 0, R + 1, 0)

    def along_tm(hop, part):
        row = cb.at[2, edge] if part == 0 else cb.at[2, pl.ds(rest, hr - 1)]
        there = cb.at[2 - hop, edge] if part == 0 else cb.at[2 - hop, pl.ds(rest, hr - 1)]
        return send(row, there, s_tm.at[hop - 1, part], r_tm.at[hop - 1, part], dev(frame=tm + hop))

    def edge_copy(f, k):
        src = cb.at[f, edge]
        if k == 0:
            return send(src, src, s_edge.at[f, 0], r_edge.at[f], dev(core=o))
        side = o
        return send(src, cb.at[f, far], s_edge.at[f, k], r_halo.at[f, side], dev(dz=near, core=k - 1))

    def rest_copy(f):
        src = cb.at[f, pl.ds(rest, hr - 1)]
        return send(src, src, s_rest.at[f], r_rest.at[f], dev(core=o))

    def from_sibling(f):
        there = jnp.where(c == 0, R, 1)
        others = jnp.where(c == 0, 1 + hr, 2)
        row = cb.at[f, there]
        send(row, row, s_edge.at[f, 0], r_edge.at[f], dev(core=o)).wait_recv()
        rows = cb.at[f, pl.ds(others, hr - 1)]
        send(rows, rows, s_rest.at[f], r_rest.at[f], dev(core=o)).wait_recv()

    def from_halo(f):
        @pl.when(z > 0)
        def _():
            row = cb.at[f, 0]
            send(row, row, s_edge.at[f, 1], r_halo.at[f, 0], dev(core=o)).wait_recv()

        @pl.when(z < Z - 1)
        def _():
            row = cb.at[f, R + 1]
            send(row, row, s_edge.at[f, 2], r_halo.at[f, 1], dev(core=o)).wait_recv()

    def spread_edge(f):
        edge_copy(f, 0).start()

        @pl.when(has_near)
        def _():
            edge_copy(f, 1).start()
            edge_copy(f, 2).start()

    for part in (0, 1):
        for hop in (1, 2):
            if N > hop:
                pl.when(tm + hop < N)(along_tm(hop, part).start)
        if part == 0:
            spread_edge(2)
        else:
            rest_copy(2).start()

    low, high = joined[:, :S].astype(BF16), joined[:, S:].astype(BF16)
    jo[pl.ds(c * hr, hr)] = jnp.where(c == 0, low, high).reshape(hr, W, S)
    jt[...] = jnp.where(c == 0, high, low).reshape(hr, W, S)
    joined_copy = send(jt, jo.at[pl.ds(c * hr, hr)], s_pair.at[1], r_pair.at[1], dev(core=o))
    joined_copy.start()

    def taps(f, start):
        rows = jnp.concatenate([cb[f, dh : dh + R].reshape(T, C) for dh in range(3)], axis=-1)
        for dw in range(3):
            value = jnp.dot(rows, cw[f, :, dw].reshape(3 * C, S), preferred_element_type=F32)
            if start:
                parts[dw, pl.ds(8, T)] = value
            else:
                parts[dw, pl.ds(8, T)] += value

    def forwarded(f):
        hop = 2 - f

        def run():
            for part in (0, 1):
                along_tm(hop, part).wait_recv()
                if part == 0:
                    spread_edge(f)
                else:
                    rest_copy(f).start()

        return run

    weights[4].wait()
    pl.when(tm <= 1)(cache_two.wait)
    from_sibling(2)
    from_halo(2)
    taps(2, True)
    if N > 2:
        pl.when(tm >= 2)(forwarded(0))
        pl.when(tm >= 2)(lambda: from_sibling(0))
    pl.when(tm >= 1)(forwarded(1))
    from_halo(0)
    taps(0, False)
    pl.when(tm == 0)(cache_one.wait)
    pl.when(tm >= 1)(lambda: from_sibling(1))
    from_halo(1)
    taps(1, False)

    there = jo.at[pl.ds(o * hr, hr)]
    send(jt, there, s_pair.at[1], r_pair.at[1], dev(core=o)).wait_recv()
    cell = lax.rem(lax.broadcasted_iota(jnp.int32, (T, S), 0), W)
    before = jnp.where(cell == 0, 0.0, parts[0, pl.ds(7, T)])
    after = jnp.where(cell == W - 1, 0.0, parts[2, pl.ds(9, T)])
    conv = before + parts[1, pl.ds(8, T)] + after
    out_ref[0] = (jo[...].reshape(T, S).astype(F32) + conv).astype(BF16).reshape(R, W, S)

    pair.wait_send()
    joined_copy.wait_send()
    pl.when(z < Z - 1)(rightward(z).wait_send)
    pl.when(z > 0)(leftward(z).wait_send)
    sideward(z).wait_send()

    def finish(d, carry):
        lo, hi = z - d, z + d

        @pl.when(lo >= 0)
        def _():
            pl.when(z < Z - 1)(rightward(lo).wait_send)
            sideward(lo).wait_send()

        @pl.when(hi < Z)
        def _():
            pl.when(z > 0)(leftward(hi).wait_send)
            sideward(hi).wait_send()

        return carry

    lax.fori_loop(1, Z, finish, 0)
    cache_edges(lambda copy: copy.wait_send())
    for part in (0, 1):
        for hop in (1, 2):
            if N > hop:
                pl.when(tm + hop < N)(along_tm(hop, part).wait_send)

    def spread_done(f):
        edge_copy(f, 0).wait_send()
        rest_copy(f).wait_send()

        @pl.when(has_near)
        def _():
            edge_copy(f, 1).wait_send()
            edge_copy(f, 2).wait_send()

    spread_done(2)
    pl.when(tm >= 1)(lambda: spread_done(1))
    if N > 2:
        pl.when(tm >= 2)(lambda: spread_done(0))


def solution(mesh):
    Z, N = mesh.shape["space"], mesh.shape["tm"]

    def body(frames_in, cache, gain_one, gain_two, w_query, w_key, w_value, w_out, conv_weight):
        _, R, W, S = frames_in.shape
        C = 2 * S
        hr, half, T = R // 2, R // 2 * W, R * W
        dma = pltpu.SemaphoreType.DMA
        hbm = pl.BlockSpec(memory_space=pl.ANY)
        vmem = pl.BlockSpec(memory_space=pltpu.VMEM)
        return pl.pallas_call(
            functools.partial(kernel, Z, N),
            out_shape=jax.ShapeDtypeStruct(frames_in.shape, BF16),
            in_specs=[hbm, hbm, vmem, vmem, hbm, hbm, hbm, hbm, hbm],
            out_specs=vmem,
            scratch_shapes=[
                pltpu.VMEM((2, hr, W, S), BF16),
                pltpu.VMEM((Z, 2, half, C), BF16),
                pltpu.VMEM((half, C), BF16),
                pltpu.VMEM((half, 1), F32),
                pltpu.VMEM((half, 1), F32),
                pltpu.VMEM((half, C), F32),
                pltpu.VMEM((3, R + 2, W, C), BF16),
                pltpu.VMEM((hr, W, S), BF16),
                pltpu.VMEM((R, W, S), BF16),
                pltpu.VMEM((3, T + 16, S), F32),
                pltpu.VMEM((C, C), BF16),
                pltpu.VMEM((C, C), BF16),
                pltpu.VMEM((C, C), BF16),
                pltpu.VMEM((C, C), BF16),
                pltpu.VMEM(conv_weight.shape, BF16),
                dma((8,)),
                dma((2,)),
                dma((2,)),
                dma((Z,)),
                dma((Z,)),
                dma((Z,)),
                dma((Z,)),
                dma((Z,)),
                dma((2, 2)),
                dma((3, 2)),
                dma((3, 3)),
                dma((3,)),
                dma((3,)),
                dma((3,)),
                dma((2, 2)),
                dma((2, 2)),
            ],
            compiler_params=pltpu.CompilerParams(
                collective_id=0, has_side_effects=True, vmem_limit_bytes=50 << 20
            ),
        )(
            frames_in, cache, gain_one.reshape(1, C), gain_two.reshape(1, C),
            w_query, w_key, w_value, w_out, conv_weight,
        )

    return jax.shard_map(
        body,
        mesh=mesh,
        in_specs=(
            P(("clips", "tm"), "space", None, "chan"),
            P("clips", "space", None, None),
            P(),
            P(),
            P(),
            P(),
            P(),
            P(),
            P(None, None, None, None, "chan"),
        ),
        out_specs=P(("clips", "tm"), "space", None, "chan"),
        check_vma=False,
    )
```

```python
import functools
import math

import jax
import jax.numpy as jnp
from jax import lax
from jax.experimental import pallas as pl
from jax.experimental.pallas import tpu as pltpu
from jax.sharding import PartitionSpec as P

F32 = jnp.float32
BF16 = jnp.bfloat16
MESH = pl.DeviceIdType.MESH


def normalized(wide, gain):
    factor = lax.rsqrt(jnp.mean(wide * wide, axis=-1, keepdims=True) + 1e-06)
    return wide * factor * gain.astype(F32).reshape(1, -1)


def kernel(
    Z, N,
    x_hbm, cache_hbm, g1_hbm, g2_hbm, wq_hbm, wk_hbm, wv_hbm, wo_hbm, cw_hbm,
    out_ref,
    xr, xg, qk, top, total, acc, cb, jt, jo, parts, g1_ref, g2_ref, wq, wk, wv, wo, cw,
    s_loc, s_pair, r_pair, s_right, s_left, s_sib, r_z, r_sib,
    s_cache, r_halo, s_edge, s_rest, r_edge, r_rest, s_tm, r_tm,
):
    z = lax.axis_index("space")
    c = lax.axis_index("chan")
    tm = lax.axis_index("tm")
    o = 1 - c
    R, W, S = out_ref.shape[1:]
    C = 2 * S
    hr = R // 2
    half = hr * W
    T = R * W

    def dev(dz=None, core=None, frame=None):
        return {
            "space": z if dz is None else dz,
            "chan": c if core is None else core,
            "tm": tm if frame is None else frame,
        }

    def send(src, dst, ssem, rsem, to):
        return pltpu.make_async_remote_copy(
            src_ref=src, dst_ref=dst, send_sem=ssem, recv_sem=rsem,
            device_id=to, device_id_type=MESH,
        )

    near = z + 2 * c - 1
    has_near = jnp.logical_and(near >= 0, near < Z)

    barrier = pltpu.get_barrier_semaphore()

    def greet(to):
        pl.semaphore_signal(barrier, inc=1, device_id=to, device_id_type=MESH)

    greet(dev(core=o))
    pl.when(z > 0)(lambda: greet(dev(dz=z - 1)))
    pl.when(z < Z - 1)(lambda: greet(dev(dz=z + 1)))
    pl.when(has_near)(lambda: greet(dev(dz=near, core=o)))
    for hop in (1, 2):
        if N > hop:
            pl.when(tm >= hop)(functools.partial(lambda h: greet(dev(frame=tm - h)), hop))

    x_own = pltpu.make_async_copy(x_hbm.at[0, pl.ds(c * hr, hr)], xr.at[c], s_loc.at[0])
    x_own.start()
    pieces = (
        (g1_hbm, g1_ref), (wq_hbm, wq), (wk_hbm, wk), (wv_hbm, wv), (wo_hbm, wo), (g2_hbm, g2_ref),
        (cw_hbm, cw),
    )
    weights = [
        pltpu.make_async_copy(a, b, s_loc.at[1 + i])
        for i, (a, b) in enumerate(pieces)
    ]
    for w in weights:
        w.start()
    first = jnp.minimum(tm, 1)
    cache_two = pltpu.make_async_copy(cache_hbm.at[first], cb.at[0, pl.ds(1, R)], s_loc.at[8])
    cache_one = pltpu.make_async_copy(cache_hbm.at[1], cb.at[1, pl.ds(1, R)], s_loc.at[9])
    pl.when(tm <= 1)(cache_two.start)
    pl.when(tm == 0)(cache_one.start)

    want = 1 + jnp.where(z > 0, 1, 0) + jnp.where(z < Z - 1, 1, 0) + jnp.where(has_near, 1, 0)
    for hop in (1, 2):
        if N > hop:
            want = want + jnp.where(tm + hop < N, 1, 0)
    pl.semaphore_wait(barrier, want)

    pair = send(x_hbm.at[0, pl.ds(o * hr, hr)], xr.at[c], s_pair.at[0], r_pair.at[0], dev(core=o))
    pair.start()

    blank = jnp.zeros((W, C), BF16)

    @pl.when(z == 0)
    def _():
        for f in range(3):
            cb[f, 0] = blank

    @pl.when(z == Z - 1)
    def _():
        for f in range(3):
            cb[f, R + 1] = blank

    x_own.wait()
    weights[0].wait()
    pair.wait_recv()

    def tokens():
        return jnp.concatenate(
            [xr[0].reshape(half, S).astype(F32), xr[1].reshape(half, S).astype(F32)], axis=-1
        )

    normed = normalized(tokens(), g1_ref[...]).astype(BF16)
    xg[z, c] = normed

    def rightward(j):
        return send(xg.at[j, c], xg.at[j, c], s_right.at[j], r_z.at[j], dev(dz=z + 1))

    def leftward(j):
        return send(xg.at[j, c], xg.at[j, c], s_left.at[j], r_z.at[j], dev(dz=z - 1))

    def sideward(j):
        return send(xg.at[j, c], xg.at[j, c], s_sib.at[j], r_sib.at[j], dev(core=o))

    pl.when(z < Z - 1)(rightward(z).start)
    pl.when(z > 0)(leftward(z).start)
    sideward(z).start()

    for w in weights[1:3]:
        w.wait()
    query = jnp.dot(normed, wq[...], preferred_element_type=F32).astype(BF16)
    folded = lax.dot_general(query, wk[...], (((1,), (1,)), ((), ())), preferred_element_type=F32)
    qk[...] = (folded * (C ** (-0.5) * math.log2(math.e))).astype(BF16)
    top[...] = jnp.full(top.shape, -1e30, F32)
    total[...] = jnp.zeros(total.shape, F32)
    acc[...] = jnp.zeros(acc.shape, F32)

    def attend(j):
        keys = xg[j].reshape(T, C)
        scores = lax.dot_general(qk[...], keys, (((1,), (1,)), ((), ())), preferred_element_type=F32)
        old = top[...]
        new = jnp.maximum(old, jnp.max(scores, axis=-1, keepdims=True))
        weight = jnp.exp2(scores - new)
        fade = jnp.exp2(old - new)
        top[...] = new
        total[...] = total[...] * fade + jnp.sum(weight, axis=-1, keepdims=True)
        acc[...] = acc[...] * fade + jnp.dot(weight.astype(BF16), keys, preferred_element_type=F32)

    sideward(z).wait_recv()
    attend(z)

    def cache_edge(f, side):
        row = R - 1 if side == 0 else 0
        source = cache_hbm.at[first if f == 0 else 1, row]
        to = dev(dz=z + 1) if side == 0 else dev(dz=z - 1)
        return send(source, cb.at[f, 0 if side == 0 else R + 1], s_cache.at[f, side], r_halo.at[f, side], to)

    def cache_edges(act):
        for side, there in ((0, z < Z - 1), (1, z > 0)):
            pl.when(jnp.logical_and(there, tm <= 1))(lambda s=side: act(cache_edge(0, s)))
            pl.when(jnp.logical_and(there, tm == 0))(lambda s=side: act(cache_edge(1, s)))

    def step(d, carry):
        lo, hi = z - d, z + d
        has_lo, has_hi = lo >= 0, hi < Z

        @pl.when(has_lo)
        def _():
            rightward(lo).wait_recv()
            pl.when(z < Z - 1)(rightward(lo).start)
            sideward(lo).start()

        @pl.when(has_hi)
        def _():
            leftward(hi).wait_recv()
            pl.when(z > 0)(leftward(hi).start)
            sideward(hi).start()

        pl.when(d == Z - 1)(lambda: cache_edges(lambda copy: copy.start()))

        @pl.when(has_lo)
        def _():
            sideward(lo).wait_recv()
            attend(lo)

        @pl.when(has_hi)
        def _():
            sideward(hi).wait_recv()
            attend(hi)

        return carry

    lax.fori_loop(1, Z, step, 0)

    for w in weights[3:6]:
        w.wait()
    mixed = (acc[...] * (1.0 / total[...])).astype(BF16)
    attended = jnp.dot(mixed, wv[...], preferred_element_type=F32).astype(BF16)
    joined = tokens() + jnp.dot(attended, wo[...], preferred_element_type=F32)
    joined = joined.astype(BF16).astype(F32)
    scaled = normalized(joined, g2_ref[...])
    act = (scaled / (1.0 + jnp.exp(-scaled))).astype(BF16)
    mine = 1 + c * hr
    cb[2, pl.ds(mine, hr)] = act.reshape(hr, W, C)

    edge = jnp.where(c == 0, 1, R)
    rest = jnp.where(c == 0, 2, 1 + hr)
    far = jnp.where(c == 0, R + 1, 0)

    def along_tm(hop, part):
        row = cb.at[2, edge] if part == 0 else cb.at[2, pl.ds(rest, hr - 1)]
        there = cb.at[2 - hop, edge] if part == 0 else cb.at[2 - hop, pl.ds(rest, hr - 1)]
        return send(row, there, s_tm.at[hop - 1, part], r_tm.at[hop - 1, part], dev(frame=tm + hop))

    def edge_copy(f, k):
        src = cb.at[f, edge]
        if k == 0:
            return send(src, src, s_edge.at[f, 0], r_edge.at[f], dev(core=o))
        side = o
        return send(src, cb.at[f, far], s_edge.at[f, k], r_halo.at[f, side], dev(dz=near, core=k - 1))

    def rest_copy(f):
        src = cb.at[f, pl.ds(rest, hr - 1)]
        return send(src, src, s_rest.at[f], r_rest.at[f], dev(core=o))

    def from_sibling(f):
        there = jnp.where(c == 0, R, 1)
        others = jnp.where(c == 0, 1 + hr, 2)
        row = cb.at[f, there]
        send(row, row, s_edge.at[f, 0], r_edge.at[f], dev(core=o)).wait_recv()
        rows = cb.at[f, pl.ds(others, hr - 1)]
        send(rows, rows, s_rest.at[f], r_rest.at[f], dev(core=o)).wait_recv()

    def from_halo(f):
        @pl.when(z > 0)
        def _():
            row = cb.at[f, 0]
            send(row, row, s_edge.at[f, 1], r_halo.at[f, 0], dev(core=o)).wait_recv()

        @pl.when(z < Z - 1)
        def _():
            row = cb.at[f, R + 1]
            send(row, row, s_edge.at[f, 2], r_halo.at[f, 1], dev(core=o)).wait_recv()

    def spread_edge(f):
        edge_copy(f, 0).start()

        @pl.when(has_near)
        def _():
            edge_copy(f, 1).start()
            edge_copy(f, 2).start()

    for part in (0, 1):
        for hop in (1, 2):
            if N > hop:
                pl.when(tm + hop < N)(along_tm(hop, part).start)
        if part == 0:
            spread_edge(2)
        else:
            rest_copy(2).start()

    low, high = joined[:, :S].astype(BF16), joined[:, S:].astype(BF16)
    jo[pl.ds(c * hr, hr)] = jnp.where(c == 0, low, high).reshape(hr, W, S)
    jt[...] = jnp.where(c == 0, high, low).reshape(hr, W, S)
    joined_copy = send(jt, jo.at[pl.ds(c * hr, hr)], s_pair.at[1], r_pair.at[1], dev(core=o))
    joined_copy.start()

    def taps(f, start):
        rows = jnp.concatenate([cb[f, dh : dh + R].reshape(T, C) for dh in range(3)], axis=-1)
        for dw in range(3):
            kernel_rows = jnp.concatenate([cw[f, dh, dw] for dh in range(3)], axis=-1)
            value = lax.dot_general(
                rows, kernel_rows, (((1,), (1,)), ((), ())), preferred_element_type=F32
            )
            if start:
                parts[dw, pl.ds(8, T)] = value
            else:
                parts[dw, pl.ds(8, T)] += value

    def forwarded(f):
        hop = 2 - f

        def run():
            for part in (0, 1):
                along_tm(hop, part).wait_recv()
                if part == 0:
                    spread_edge(f)
                else:
                    rest_copy(f).start()

        return run

    weights[6].wait()
    pl.when(tm <= 1)(cache_two.wait)
    from_sibling(2)
    from_halo(2)
    taps(2, True)
    if N > 2:
        pl.when(tm >= 2)(forwarded(0))
        pl.when(tm >= 2)(lambda: from_sibling(0))
    pl.when(tm >= 1)(forwarded(1))
    from_halo(0)
    taps(0, False)
    pl.when(tm == 0)(cache_one.wait)
    pl.when(tm >= 1)(lambda: from_sibling(1))
    from_halo(1)
    taps(1, False)

    there = jo.at[pl.ds(o * hr, hr)]
    send(jt, there, s_pair.at[1], r_pair.at[1], dev(core=o)).wait_recv()
    cell = lax.rem(lax.broadcasted_iota(jnp.int32, (T, S), 0), W)
    before = jnp.where(cell == 0, 0.0, parts[0, pl.ds(7, T)])
    after = jnp.where(cell == W - 1, 0.0, parts[2, pl.ds(9, T)])
    conv = before + parts[1, pl.ds(8, T)] + after
    out_ref[0] = (jo[...].reshape(T, S).astype(F32) + conv).astype(BF16).reshape(R, W, S)

    pair.wait_send()
    joined_copy.wait_send()
    pl.when(z < Z - 1)(rightward(z).wait_send)
    pl.when(z > 0)(leftward(z).wait_send)
    sideward(z).wait_send()

    def finish(d, carry):
        lo, hi = z - d, z + d

        @pl.when(lo >= 0)
        def _():
            pl.when(z < Z - 1)(rightward(lo).wait_send)
            sideward(lo).wait_send()

        @pl.when(hi < Z)
        def _():
            pl.when(z > 0)(leftward(hi).wait_send)
            sideward(hi).wait_send()

        return carry

    lax.fori_loop(1, Z, finish, 0)
    cache_edges(lambda copy: copy.wait_send())
    for part in (0, 1):
        for hop in (1, 2):
            if N > hop:
                pl.when(tm + hop < N)(along_tm(hop, part).wait_send)

    def spread_done(f):
        edge_copy(f, 0).wait_send()
        rest_copy(f).wait_send()

        @pl.when(has_near)
        def _():
            edge_copy(f, 1).wait_send()
            edge_copy(f, 2).wait_send()

    spread_done(2)
    pl.when(tm >= 1)(lambda: spread_done(1))
    if N > 2:
        pl.when(tm >= 2)(lambda: spread_done(0))


def solution(mesh):
    Z, N = mesh.shape["space"], mesh.shape["tm"]

    def body(frames_in, cache, gain_one, gain_two, w_query, w_key, w_value, w_out, conv_weight):
        _, R, W, S = frames_in.shape
        C = 2 * S
        hr, half, T = R // 2, R // 2 * W, R * W
        dma = pltpu.SemaphoreType.DMA
        hbm = pl.BlockSpec(memory_space=pltpu.HBM)
        vmem = pl.BlockSpec(memory_space=pltpu.VMEM)
        return pl.pallas_call(
            functools.partial(kernel, Z, N),
            out_shape=jax.ShapeDtypeStruct(frames_in.shape, BF16),
            in_specs=[hbm] * 9,
            out_specs=vmem,
            scratch_shapes=[
                pltpu.VMEM((2, hr, W, S), BF16),
                pltpu.VMEM((Z, 2, half, C), BF16),
                pltpu.VMEM((half, C), BF16),
                pltpu.VMEM((half, 1), F32),
                pltpu.VMEM((half, 1), F32),
                pltpu.VMEM((half, C), F32),
                pltpu.VMEM((3, R + 2, W, C), BF16),
                pltpu.VMEM((hr, W, S), BF16),
                pltpu.VMEM((R, W, S), BF16),
                pltpu.VMEM((3, T + 16, S), F32),
                pltpu.VMEM((C,), BF16),
                pltpu.VMEM((C,), BF16),
                pltpu.VMEM((C, C), BF16),
                pltpu.VMEM((C, C), BF16),
                pltpu.VMEM((C, C), BF16),
                pltpu.VMEM((C, C), BF16),
                pltpu.VMEM((3, 3, 3, S, C), BF16),
                dma((10,)),
                dma((2,)),
                dma((2,)),
                dma((Z,)),
                dma((Z,)),
                dma((Z,)),
                dma((Z,)),
                dma((Z,)),
                dma((2, 2)),
                dma((3, 2)),
                dma((3, 3)),
                dma((3,)),
                dma((3,)),
                dma((3,)),
                dma((2, 2)),
                dma((2, 2)),
            ],
            compiler_params=pltpu.CompilerParams(
                collective_id=0, has_side_effects=True, vmem_limit_bytes=63 << 20
            ),
        )(
            frames_in, cache, gain_one, gain_two,
            w_query, w_key, w_value, w_out, jnp.swapaxes(conv_weight, 3, 4),
        )

    return jax.shard_map(
        body,
        mesh=mesh,
        in_specs=(
            P(("clips", "tm"), "space", None, "chan"),
            P("clips", "space", None, None),
            P(),
            P(),
            P(),
            P(),
            P(),
            P(),
            P(None, None, None, None, "chan"),
        ),
        out_specs=P(("clips", "tm"), "space", None, "chan"),
        check_vma=False,
    )
```

```python
import functools
import math

import jax
import jax.numpy as jnp
from jax import lax
from jax.experimental import pallas as pl
from jax.experimental.pallas import tpu as pltpu
from jax.sharding import PartitionSpec as P

F32 = jnp.float32
BF16 = jnp.bfloat16
MESH = pl.DeviceIdType.MESH


def normalized(wide, gain):
    factor = lax.rsqrt(jnp.mean(wide * wide, axis=-1, keepdims=True) + 1e-06)
    return wide * factor * gain.astype(F32).reshape(1, -1)


def kernel(
    Z, N,
    x_hbm, cache_hbm, g1_hbm, g2_hbm, wq_hbm, wk_hbm, wv_hbm, wo_hbm, cw_hbm,
    out_ref,
    xr, xg, qk, top, total, acc, cb, jt, jo, parts, g1_ref, g2_ref, wq, wk, wv, wo, cw,
    s_loc, s_pair, r_pair, s_right, s_left, s_sib, r_z, r_sib,
    s_cache, r_halo, s_edge, s_rest, r_edge, r_rest, s_tm, r_tm, s_half, r_half,
):
    z = lax.axis_index("space")
    c = lax.axis_index("chan")
    tm = lax.axis_index("tm")
    o = 1 - c
    R, W, S = out_ref.shape[1:]
    C = 2 * S
    hr = R // 2
    half = hr * W
    T = R * W
    hw = W // 2

    def dev(dz=None, core=None, frame=None):
        return {
            "space": z if dz is None else dz,
            "chan": c if core is None else core,
            "tm": tm if frame is None else frame,
        }

    def send(src, dst, ssem, rsem, to):
        return pltpu.make_async_remote_copy(
            src_ref=src, dst_ref=dst, send_sem=ssem, recv_sem=rsem,
            device_id=to, device_id_type=MESH,
        )

    near = z + 2 * c - 1
    has_near = jnp.logical_and(near >= 0, near < Z)

    barrier = pltpu.get_barrier_semaphore()

    def greet(to):
        pl.semaphore_signal(barrier, inc=1, device_id=to, device_id_type=MESH)

    greet(dev(core=o))
    pl.when(z > 0)(lambda: greet(dev(dz=z - 1)))
    pl.when(z < Z - 1)(lambda: greet(dev(dz=z + 1)))
    pl.when(has_near)(lambda: greet(dev(dz=near, core=o)))
    for hop in (1, 2):
        if N > hop:
            pl.when(tm >= hop)(functools.partial(lambda h: greet(dev(frame=tm - h)), hop))

    x_own = pltpu.make_async_copy(x_hbm.at[0, pl.ds(c * hr, hr)], xr.at[c], s_loc.at[0])
    x_own.start()
    pieces = (
        (g1_hbm, g1_ref), (wq_hbm, wq), (wk_hbm, wk), (wv_hbm, wv), (wo_hbm, wo), (g2_hbm, g2_ref),
        (cw_hbm, cw),
    )
    weights = [
        pltpu.make_async_copy(a, b, s_loc.at[1 + i])
        for i, (a, b) in enumerate(pieces)
    ]
    for w in weights:
        w.start()
    first = jnp.minimum(tm, 1)
    cache_two = pltpu.make_async_copy(cache_hbm.at[first], cb.at[0, pl.ds(1, R)], s_loc.at[8])
    cache_one = pltpu.make_async_copy(cache_hbm.at[1], cb.at[1, pl.ds(1, R)], s_loc.at[9])
    pl.when(tm <= 1)(cache_two.start)
    pl.when(tm == 0)(cache_one.start)

    want = 1 + jnp.where(z > 0, 1, 0) + jnp.where(z < Z - 1, 1, 0) + jnp.where(has_near, 1, 0)
    for hop in (1, 2):
        if N > hop:
            want = want + jnp.where(tm + hop < N, 1, 0)
    pl.semaphore_wait(barrier, want)

    pair = send(x_hbm.at[0, pl.ds(o * hr, hr)], xr.at[c], s_pair.at[0], r_pair.at[0], dev(core=o))
    pair.start()

    blank = jnp.zeros((W, C), BF16)

    @pl.when(z == 0)
    def _():
        for f in range(3):
            cb[f, 0] = blank

    @pl.when(z == Z - 1)
    def _():
        for f in range(3):
            cb[f, R + 1] = blank

    x_own.wait()
    weights[0].wait()
    pair.wait_recv()

    def tokens(row, count):
        at = pl.ds(row, count)
        return jnp.concatenate(
            [xr[k, at].reshape(count * W, S).astype(F32) for k in range(2)], axis=-1
        )

    normed = normalized(tokens(0, hr), g1_ref[...]).astype(BF16)
    xg[z, c] = normed.reshape(hr, W, C)

    def rightward(j, r):
        return send(xg.at[j, c, r], xg.at[j, c, r], s_right.at[j, r], r_z.at[j, r], dev(dz=z + 1))

    def leftward(j, r):
        return send(xg.at[j, c, r], xg.at[j, c, r], s_left.at[j, r], r_z.at[j, r], dev(dz=z - 1))

    def sideward(j, r):
        return send(xg.at[j, c, r], xg.at[j, c, r], s_sib.at[j, r], r_sib.at[j, r], dev(core=o))

    for r in range(hr):
        pl.when(z < Z - 1)(rightward(z, r).start)
        pl.when(z > 0)(leftward(z, r).start)
    for r in range(hr):
        sideward(z, r).start()

    for w in weights[1:3]:
        w.wait()
    query = jnp.dot(normed, wq[...], preferred_element_type=F32).astype(BF16)
    folded = lax.dot_general(query, wk[...], (((1,), (1,)), ((), ())), preferred_element_type=F32)
    qk[...] = (folded * (C ** (-0.5) * math.log2(math.e))).astype(BF16)
    top[...] = jnp.full(top.shape, -1e30, F32)
    total[...] = jnp.zeros(total.shape, F32)
    acc[...] = jnp.zeros(acc.shape, F32)

    def attend(j):
        keys = xg[j].reshape(T, C)
        scores = lax.dot_general(qk[...], keys, (((1,), (1,)), ((), ())), preferred_element_type=F32)
        old = top[...]
        new = jnp.maximum(old, jnp.max(scores, axis=-1, keepdims=True))
        weight = jnp.exp2(scores - new)
        fade = jnp.exp2(old - new)
        top[...] = new
        total[...] = total[...] * fade + jnp.sum(weight, axis=-1, keepdims=True)
        acc[...] = acc[...] * fade + jnp.dot(weight.astype(BF16), keys, preferred_element_type=F32)

    for r in range(hr):
        sideward(z, r).wait_recv()
    attend(z)

    def cache_edge(f, side):
        row = R - 1 if side == 0 else 0
        cells = pl.ds(pl.multiple_of(c * hw, hw), hw)
        source = cache_hbm.at[first if f == 0 else 1, row, cells]
        to = dev(dz=z + 1) if side == 0 else dev(dz=z - 1)
        return send(source, cb.at[f, 0 if side == 0 else R + 1, cells], s_cache.at[f, side], r_halo.at[f, side], to)

    def cache_edges(act):
        for side, there in ((0, z < Z - 1), (1, z > 0)):
            pl.when(jnp.logical_and(there, tm <= 1))(lambda s=side: act(cache_edge(0, s)))
            pl.when(jnp.logical_and(there, tm == 0))(lambda s=side: act(cache_edge(1, s)))

    def step(d, carry):
        lo, hi = z - d, z + d
        has_lo, has_hi = lo >= 0, hi < Z

        for r in range(hr):

            @pl.when(has_lo)
            def _():
                rightward(lo, r).wait_recv()
                pl.when(z < Z - 1)(rightward(lo, r).start)
                sideward(lo, r).start()

            @pl.when(has_hi)
            def _():
                leftward(hi, r).wait_recv()
                pl.when(z > 0)(leftward(hi, r).start)
                sideward(hi, r).start()

        pl.when(d == Z - 1)(lambda: cache_edges(lambda copy: copy.start()))

        @pl.when(has_lo)
        def _():
            for r in range(hr):
                sideward(lo, r).wait_recv()
            attend(lo)

        @pl.when(has_hi)
        def _():
            for r in range(hr):
                sideward(hi, r).wait_recv()
            attend(hi)

        return carry

    lax.fori_loop(1, Z, step, 0)

    for w in weights[3:6]:
        w.wait()
    def finish_rows(row, count):
        at = pl.ds(pl.multiple_of(row * W, W), count * W)
        mixed = (acc[at, :] * (1.0 / total[at, :])).astype(BF16)
        attended = jnp.dot(mixed, wv[...], preferred_element_type=F32).astype(BF16)
        joined = tokens(row, count) + jnp.dot(attended, wo[...], preferred_element_type=F32)
        joined = joined.astype(BF16).astype(F32)
        scaled = normalized(joined, g2_ref[...])
        act = (scaled / (1.0 + jnp.exp(-scaled))).astype(BF16)
        cb[2, pl.ds(1 + c * hr + row, count)] = act.reshape(count, W, C)
        low, high = joined[:, :S].astype(BF16), joined[:, S:].astype(BF16)
        jo[pl.ds(c * hr + row, count)] = jnp.where(c == 0, low, high).reshape(count, W, S)
        jt[pl.ds(row, count)] = jnp.where(c == 0, high, low).reshape(count, W, S)

    edge = jnp.where(c == 0, 1, R)
    rest = jnp.where(c == 0, 2, 1 + hr)
    far = jnp.where(c == 0, R + 1, 0)

    def along_tm(hop, part):
        row = cb.at[2, edge] if part == 0 else cb.at[2, pl.ds(rest, hr - 1)]
        there = cb.at[2 - hop, edge] if part == 0 else cb.at[2 - hop, pl.ds(rest, hr - 1)]
        return send(row, there, s_tm.at[hop - 1, part], r_tm.at[hop - 1, part], dev(frame=tm + hop))

    def edge_copy(f, k):
        src = cb.at[f, edge]
        if k == 0:
            return send(src, src, s_edge.at[f, 0], r_edge.at[f], dev(core=o))
        cells = pl.ds((k - 1) * hw, hw)
        return send(
            cb.at[f, edge, cells], cb.at[f, far, cells], s_edge.at[f, k], r_halo.at[f, o],
            dev(dz=near, core=k - 1),
        )

    def rest_copy(f):
        src = cb.at[f, pl.ds(rest, hr - 1)]
        return send(src, src, s_rest.at[f], r_rest.at[f], dev(core=o))

    def from_sibling(f):
        there = jnp.where(c == 0, R, 1)
        others = jnp.where(c == 0, 1 + hr, 2)
        row = cb.at[f, there]
        send(row, row, s_edge.at[f, 0], r_edge.at[f], dev(core=o)).wait_recv()
        rows = cb.at[f, pl.ds(others, hr - 1)]
        send(rows, rows, s_rest.at[f], r_rest.at[f], dev(core=o)).wait_recv()

    def halo_half(f, side, core):
        half_row = cb.at[f, 0 if side == 0 else R + 1, pl.ds(pl.multiple_of(core * hw, hw), hw)]
        return send(half_row, half_row, s_half.at[f, side], r_half.at[f, side], dev(core=o))

    def both_sides(visit):
        pl.when(z > 0)(lambda: visit(0))
        pl.when(z < Z - 1)(lambda: visit(1))

    def relay_halo(f):
        def visit(side):
            half_row = cb.at[f, 0 if side == 0 else R + 1, pl.ds(pl.multiple_of(c * hw, hw), hw)]
            send(half_row, half_row, s_edge.at[f, 1], r_halo.at[f, side], dev(core=o)).wait_recv()
            halo_half(f, side, c).start()

        both_sides(visit)

    def from_halo(f):
        both_sides(lambda side: halo_half(f, side, o).wait_recv())

    def spread_edge(f):
        edge_copy(f, 0).start()

        @pl.when(has_near)
        def _():
            edge_copy(f, 1).start()
            edge_copy(f, 2).start()

    for part in (0, 1):
        if part == 0:
            finish_rows(edge - 1 - c * hr, 1)
        else:
            finish_rows(rest - 1 - c * hr, hr - 1)
        for hop in (1, 2):
            if N > hop:
                pl.when(tm + hop < N)(along_tm(hop, part).start)
        if part == 0:
            spread_edge(2)
        else:
            rest_copy(2).start()

    joined_copy = send(jt, jo.at[pl.ds(c * hr, hr)], s_pair.at[1], r_pair.at[1], dev(core=o))
    joined_copy.start()

    def taps(f, start):
        rows = jnp.concatenate([cb[f, dh : dh + R].reshape(T, C) for dh in range(3)], axis=-1)
        for dw in range(3):
            kernel_rows = jnp.concatenate([cw[f, dh, dw] for dh in range(3)], axis=-1)
            value = lax.dot_general(
                rows, kernel_rows, (((1,), (1,)), ((), ())), preferred_element_type=F32
            )
            if start:
                parts[dw, pl.ds(8, T)] = value
            else:
                parts[dw, pl.ds(8, T)] += value

    def forwarded(f, part):
        along_tm(2 - f, part).wait_recv()
        if part == 0:
            spread_edge(f)
        else:
            rest_copy(f).start()

    def arrived(f):
        relay_halo(f)
        from_sibling(f)

    def older():
        forwarded(0, 0)
        forwarded(0, 1)
        arrived(0)

    def newer():
        forwarded(1, 1)
        arrived(1)

    pl.when(tm <= 1)(lambda: relay_halo(0))
    pl.when(tm == 0)(lambda: relay_halo(1))
    arrived(2)
    weights[6].wait()
    pl.when(tm <= 1)(cache_two.wait)
    pl.when(tm == 0)(cache_one.wait)
    from_halo(2)
    taps(2, True)
    if N > 2:
        pl.when(tm >= 2)(older)
    pl.when(tm >= 1)(lambda: forwarded(1, 0))
    from_halo(0)
    taps(0, False)
    pl.when(tm >= 1)(newer)
    from_halo(1)
    taps(1, False)

    there = jo.at[pl.ds(o * hr, hr)]
    send(jt, there, s_pair.at[1], r_pair.at[1], dev(core=o)).wait_recv()
    cell = lax.rem(lax.broadcasted_iota(jnp.int32, (T, S), 0), W)
    before = jnp.where(cell == 0, 0.0, parts[0, pl.ds(7, T)])
    after = jnp.where(cell == W - 1, 0.0, parts[2, pl.ds(9, T)])
    conv = before + parts[1, pl.ds(8, T)] + after
    out_ref[0] = (jo[...].reshape(T, S).astype(F32) + conv).astype(BF16).reshape(R, W, S)

    pair.wait_send()
    joined_copy.wait_send()
    for r in range(hr):
        pl.when(z < Z - 1)(rightward(z, r).wait_send)
        pl.when(z > 0)(leftward(z, r).wait_send)
        sideward(z, r).wait_send()

    def finish(d, carry):
        lo, hi = z - d, z + d

        for r in range(hr):

            @pl.when(lo >= 0)
            def _():
                pl.when(z < Z - 1)(rightward(lo, r).wait_send)
                sideward(lo, r).wait_send()

            @pl.when(hi < Z)
            def _():
                pl.when(z > 0)(leftward(hi, r).wait_send)
                sideward(hi, r).wait_send()

        return carry

    lax.fori_loop(1, Z, finish, 0)
    cache_edges(lambda copy: copy.wait_send())
    for f in range(3):
        both_sides(lambda side: halo_half(f, side, c).wait_send())
    for part in (0, 1):
        for hop in (1, 2):
            if N > hop:
                pl.when(tm + hop < N)(along_tm(hop, part).wait_send)

    def spread_done(f):
        edge_copy(f, 0).wait_send()
        rest_copy(f).wait_send()

        @pl.when(has_near)
        def _():
            edge_copy(f, 1).wait_send()
            edge_copy(f, 2).wait_send()

    spread_done(2)
    pl.when(tm >= 1)(lambda: spread_done(1))
    if N > 2:
        pl.when(tm >= 2)(lambda: spread_done(0))


def solution(mesh):
    Z, N = mesh.shape["space"], mesh.shape["tm"]

    def body(frames_in, cache, gain_one, gain_two, w_query, w_key, w_value, w_out, conv_weight):
        _, R, W, S = frames_in.shape
        C = 2 * S
        hr, half, T = R // 2, R // 2 * W, R * W
        dma = pltpu.SemaphoreType.DMA
        hbm = pl.BlockSpec(memory_space=pltpu.HBM)
        vmem = pl.BlockSpec(memory_space=pltpu.VMEM)
        return pl.pallas_call(
            functools.partial(kernel, Z, N),
            out_shape=jax.ShapeDtypeStruct(frames_in.shape, BF16),
            in_specs=[hbm] * 9,
            out_specs=vmem,
            scratch_shapes=[
                pltpu.VMEM((2, hr, W, S), BF16),
                pltpu.VMEM((Z, 2, hr, W, C), BF16),
                pltpu.VMEM((half, C), BF16),
                pltpu.VMEM((half, 1), F32),
                pltpu.VMEM((half, 1), F32),
                pltpu.VMEM((half, C), F32),
                pltpu.VMEM((3, R + 2, W, C), BF16),
                pltpu.VMEM((hr, W, S), BF16),
                pltpu.VMEM((R, W, S), BF16),
                pltpu.VMEM((3, T + 16, S), F32),
                pltpu.VMEM((C,), BF16),
                pltpu.VMEM((C,), BF16),
                pltpu.VMEM((C, C), BF16),
                pltpu.VMEM((C, C), BF16),
                pltpu.VMEM((C, C), BF16),
                pltpu.VMEM((C, C), BF16),
                pltpu.VMEM((3, 3, 3, S, C), BF16),
                dma((10,)),
                dma((2,)),
                dma((2,)),
                dma((Z, hr)),
                dma((Z, hr)),
                dma((Z, hr)),
                dma((Z, hr)),
                dma((Z, hr)),
                dma((2, 2)),
                dma((3, 2)),
                dma((3, 3)),
                dma((3,)),
                dma((3,)),
                dma((3,)),
                dma((2, 2)),
                dma((2, 2)),
                dma((3, 2)),
                dma((3, 2)),
            ],
            compiler_params=pltpu.CompilerParams(
                collective_id=0, has_side_effects=True, vmem_limit_bytes=63 << 20
            ),
        )(
            frames_in, cache, gain_one, gain_two,
            w_query, w_key, w_value, w_out, jnp.swapaxes(conv_weight, 3, 4),
        )

    return jax.shard_map(
        body,
        mesh=mesh,
        in_specs=(
            P(("clips", "tm"), "space", None, "chan"),
            P("clips", "space", None, None),
            P(),
            P(),
            P(),
            P(),
            P(),
            P(),
            P(None, None, None, None, "chan"),
        ),
        out_specs=P(("clips", "tm"), "space", None, "chan"),
        check_vma=False,
    )
```

```python
import functools
import math

import jax
import jax.numpy as jnp
from jax import lax
from jax.experimental import pallas as pl
from jax.experimental.pallas import tpu as pltpu
from jax.sharding import PartitionSpec as P

F32 = jnp.float32
BF16 = jnp.bfloat16
MESH = pl.DeviceIdType.MESH


def normalized(wide, gain):
    factor = lax.rsqrt(jnp.mean(wide * wide, axis=-1, keepdims=True) + 1e-06)
    return wide * factor * gain.astype(F32).reshape(1, -1)


def kernel(
    Z, N,
    x_hbm, cache_hbm, g1_hbm, g2_hbm, wq_hbm, wk_hbm, wv_hbm, wo_hbm, cw_hbm,
    out_ref,
    xr, xg, qk, top, total, acc, cb, jt, jo, parts, g1_ref, g2_ref, wq, wk, wv, wo, cw,
    s_loc, s_pair, r_pair, s_first, r_first, s_right, s_left, s_sib, r_z, r_sib,
    s_cache, r_halo, s_edge, s_rest, r_edge, r_rest, s_tm, r_tm, s_half, r_half,
):
    z = lax.axis_index("space")
    c = lax.axis_index("chan")
    tm = lax.axis_index("tm")
    o = 1 - c
    R, W, S = out_ref.shape[1:]
    C = 2 * S
    hr = R // 2
    half = hr * W
    T = R * W
    hw = W // 2

    def dev(dz=None, core=None, frame=None):
        return {
            "space": z if dz is None else dz,
            "chan": c if core is None else core,
            "tm": tm if frame is None else frame,
        }

    def send(src, dst, ssem, rsem, to):
        return pltpu.make_async_remote_copy(
            src_ref=src, dst_ref=dst, send_sem=ssem, recv_sem=rsem,
            device_id=to, device_id_type=MESH,
        )

    near = z + 2 * c - 1
    has_near = jnp.logical_and(near >= 0, near < Z)

    barrier = pltpu.get_barrier_semaphore()

    def greet(to):
        pl.semaphore_signal(barrier, inc=1, device_id=to, device_id_type=MESH)

    greet(dev(core=o))
    pl.when(z > 0)(lambda: greet(dev(dz=z - 1)))
    pl.when(z < Z - 1)(lambda: greet(dev(dz=z + 1)))
    pl.when(has_near)(lambda: greet(dev(dz=near, core=o)))
    for hop in (1, 2):
        if N > hop:
            pl.when(tm >= hop)(functools.partial(lambda h: greet(dev(frame=tm - h)), hop))

    x_own = pltpu.make_async_copy(x_hbm.at[0, pl.ds(c * hr, hr)], xr.at[c], s_loc.at[0])
    x_own.start()
    pieces = (
        (g1_hbm, g1_ref), (wq_hbm, wq), (wk_hbm, wk), (wv_hbm, wv), (wo_hbm, wo), (g2_hbm, g2_ref),
        (cw_hbm, cw),
    )
    weights = [
        pltpu.make_async_copy(a, b, s_loc.at[1 + i])
        for i, (a, b) in enumerate(pieces)
    ]
    for w in weights:
        w.start()
    first = jnp.minimum(tm, 1)
    cache_two = pltpu.make_async_copy(cache_hbm.at[first], cb.at[0, pl.ds(1, R)], s_loc.at[8])
    cache_one = pltpu.make_async_copy(cache_hbm.at[1], cb.at[1, pl.ds(1, R)], s_loc.at[9])
    pl.when(tm <= 1)(cache_two.start)
    pl.when(tm == 0)(cache_one.start)

    want = 1 + jnp.where(z > 0, 1, 0) + jnp.where(z < Z - 1, 1, 0) + jnp.where(has_near, 1, 0)
    for hop in (1, 2):
        if N > hop:
            want = want + jnp.where(tm + hop < N, 1, 0)
    pl.semaphore_wait(barrier, want)

    def pair(r):
        return send(x_hbm.at[0, o * hr + r], xr.at[c, r], s_first.at[r], r_first.at[r], dev(core=o))

    for r in range(hr):
        pair(r).start()

    blank = jnp.zeros((W, C), BF16)

    @pl.when(z == 0)
    def _():
        for f in range(3):
            cb[f, 0] = blank

    @pl.when(z == Z - 1)
    def _():
        for f in range(3):
            cb[f, R + 1] = blank

    x_own.wait()
    weights[0].wait()
    def tokens(row, count):
        at = pl.ds(row, count)
        return jnp.concatenate(
            [xr[k, at].reshape(count * W, S).astype(F32) for k in range(2)], axis=-1
        )

    def rightward(j, r):
        return send(xg.at[j, c, r], xg.at[j, c, r], s_right.at[j, r], r_z.at[j, r], dev(dz=z + 1))

    def leftward(j, r):
        return send(xg.at[j, c, r], xg.at[j, c, r], s_left.at[j, r], r_z.at[j, r], dev(dz=z - 1))

    def sideward(j, r):
        return send(xg.at[j, c, r], xg.at[j, c, r], s_sib.at[j, r], r_sib.at[j, r], dev(core=o))

    for r in range(hr):
        pair(r).wait_recv()
        normed = normalized(tokens(r, 1), g1_ref[...]).astype(BF16)
        xg[z, c, r] = normed.reshape(W, C)
        pl.when(z < Z - 1)(rightward(z, r).start)
        pl.when(z > 0)(leftward(z, r).start)
        sideward(z, r).start()

    for w in weights[1:3]:
        w.wait()
    query = jnp.dot(xg[z, c].reshape(half, C), wq[...], preferred_element_type=F32).astype(BF16)
    folded = lax.dot_general(query, wk[...], (((1,), (1,)), ((), ())), preferred_element_type=F32)
    qk[...] = (folded * (C ** (-0.5) * math.log2(math.e))).astype(BF16)
    top[...] = jnp.full(top.shape, -1e30, F32)
    total[...] = jnp.zeros(total.shape, F32)
    acc[...] = jnp.zeros(acc.shape, F32)

    def attend(j):
        keys = xg[j].reshape(T, C)
        scores = lax.dot_general(qk[...], keys, (((1,), (1,)), ((), ())), preferred_element_type=F32)
        old = top[...]
        new = jnp.maximum(old, jnp.max(scores, axis=-1, keepdims=True))
        weight = jnp.exp2(scores - new)
        fade = jnp.exp2(old - new)
        top[...] = new
        total[...] = total[...] * fade + jnp.sum(weight, axis=-1, keepdims=True)
        acc[...] = acc[...] * fade + jnp.dot(weight.astype(BF16), keys, preferred_element_type=F32)

    for r in range(hr):
        sideward(z, r).wait_recv()
    attend(z)

    def cache_edge(f, side):
        row = R - 1 if side == 0 else 0
        cells = pl.ds(pl.multiple_of(c * hw, hw), hw)
        source = cache_hbm.at[first if f == 0 else 1, row, cells]
        to = dev(dz=z + 1) if side == 0 else dev(dz=z - 1)
        return send(source, cb.at[f, 0 if side == 0 else R + 1, cells], s_cache.at[f, side], r_halo.at[f, side], to)

    def cache_edges(act):
        for side, there in ((0, z < Z - 1), (1, z > 0)):
            pl.when(jnp.logical_and(there, tm <= 1))(lambda s=side: act(cache_edge(0, s)))
            pl.when(jnp.logical_and(there, tm == 0))(lambda s=side: act(cache_edge(1, s)))

    def step(d, carry):
        lo, hi = z - d, z + d
        has_lo, has_hi = lo >= 0, hi < Z

        for r in range(hr):

            @pl.when(has_lo)
            def _():
                rightward(lo, r).wait_recv()
                pl.when(z < Z - 1)(rightward(lo, r).start)
                sideward(lo, r).start()

            @pl.when(has_hi)
            def _():
                leftward(hi, r).wait_recv()
                pl.when(z > 0)(leftward(hi, r).start)
                sideward(hi, r).start()

        pl.when(d == Z - 1)(lambda: cache_edges(lambda copy: copy.start()))

        @pl.when(has_lo)
        def _():
            for r in range(hr):
                sideward(lo, r).wait_recv()
            attend(lo)

        @pl.when(has_hi)
        def _():
            for r in range(hr):
                sideward(hi, r).wait_recv()
            attend(hi)

        return carry

    lax.fori_loop(1, Z, step, 0)

    for w in weights[3:6]:
        w.wait()
    def finish_rows(row, count):
        at = pl.ds(pl.multiple_of(row * W, W), count * W)
        mixed = (acc[at, :] * (1.0 / total[at, :])).astype(BF16)
        attended = jnp.dot(mixed, wv[...], preferred_element_type=F32).astype(BF16)
        joined = tokens(row, count) + jnp.dot(attended, wo[...], preferred_element_type=F32)
        joined = joined.astype(BF16).astype(F32)
        scaled = normalized(joined, g2_ref[...])
        act = (scaled / (1.0 + jnp.exp(-scaled))).astype(BF16)
        cb[2, pl.ds(1 + c * hr + row, count)] = act.reshape(count, W, C)
        low, high = joined[:, :S].astype(BF16), joined[:, S:].astype(BF16)
        jo[pl.ds(c * hr + row, count)] = jnp.where(c == 0, low, high).reshape(count, W, S)
        jt[pl.ds(row, count)] = jnp.where(c == 0, high, low).reshape(count, W, S)

    edge = jnp.where(c == 0, 1, R)
    rest = jnp.where(c == 0, 2, 1 + hr)
    far = jnp.where(c == 0, R + 1, 0)

    def along_tm(hop, part):
        row = cb.at[2, edge] if part == 0 else cb.at[2, pl.ds(rest, hr - 1)]
        there = cb.at[2 - hop, edge] if part == 0 else cb.at[2 - hop, pl.ds(rest, hr - 1)]
        return send(row, there, s_tm.at[hop - 1, part], r_tm.at[hop - 1, part], dev(frame=tm + hop))

    def edge_copy(f, k):
        src = cb.at[f, edge]
        if k == 0:
            return send(src, src, s_edge.at[f, 0], r_edge.at[f], dev(core=o))
        cells = pl.ds((k - 1) * hw, hw)
        return send(
            cb.at[f, edge, cells], cb.at[f, far, cells], s_edge.at[f, k], r_halo.at[f, o],
            dev(dz=near, core=k - 1),
        )

    def rest_copy(f):
        src = cb.at[f, pl.ds(rest, hr - 1)]
        return send(src, src, s_rest.at[f], r_rest.at[f], dev(core=o))

    def from_sibling(f):
        there = jnp.where(c == 0, R, 1)
        others = jnp.where(c == 0, 1 + hr, 2)
        row = cb.at[f, there]
        send(row, row, s_edge.at[f, 0], r_edge.at[f], dev(core=o)).wait_recv()
        rows = cb.at[f, pl.ds(others, hr - 1)]
        send(rows, rows, s_rest.at[f], r_rest.at[f], dev(core=o)).wait_recv()

    def halo_half(f, side, core):
        half_row = cb.at[f, 0 if side == 0 else R + 1, pl.ds(pl.multiple_of(core * hw, hw), hw)]
        return send(half_row, half_row, s_half.at[f, side], r_half.at[f, side], dev(core=o))

    def both_sides(visit):
        pl.when(z > 0)(lambda: visit(0))
        pl.when(z < Z - 1)(lambda: visit(1))

    def relay_halo(f):
        def visit(side):
            half_row = cb.at[f, 0 if side == 0 else R + 1, pl.ds(pl.multiple_of(c * hw, hw), hw)]
            send(half_row, half_row, s_edge.at[f, 1], r_halo.at[f, side], dev(core=o)).wait_recv()
            halo_half(f, side, c).start()

        both_sides(visit)

    def from_halo(f):
        both_sides(lambda side: halo_half(f, side, o).wait_recv())

    def spread_edge(f):
        edge_copy(f, 0).start()

        @pl.when(has_near)
        def _():
            edge_copy(f, 1).start()
            edge_copy(f, 2).start()

    for part in (0, 1):
        if part == 0:
            finish_rows(edge - 1 - c * hr, 1)
        else:
            finish_rows(rest - 1 - c * hr, hr - 1)
        for hop in (1, 2):
            if N > hop:
                pl.when(tm + hop < N)(along_tm(hop, part).start)
        if part == 0:
            spread_edge(2)
        else:
            rest_copy(2).start()

    joined_copy = send(jt, jo.at[pl.ds(c * hr, hr)], s_pair, r_pair, dev(core=o))
    joined_copy.start()

    def taps(f, start):
        rows = jnp.concatenate([cb[f, dh : dh + R].reshape(T, C) for dh in range(3)], axis=-1)
        for dw in range(3):
            kernel_rows = jnp.concatenate([cw[f, dh, dw] for dh in range(3)], axis=-1)
            value = lax.dot_general(
                rows, kernel_rows, (((1,), (1,)), ((), ())), preferred_element_type=F32
            )
            if start:
                parts[dw, pl.ds(8, T)] = value
            else:
                parts[dw, pl.ds(8, T)] += value

    def forwarded(f, part):
        along_tm(2 - f, part).wait_recv()
        if part == 0:
            spread_edge(f)
        else:
            rest_copy(f).start()

    def arrived(f):
        relay_halo(f)
        from_sibling(f)

    def older():
        forwarded(0, 0)
        forwarded(0, 1)
        arrived(0)

    def newer():
        forwarded(1, 1)
        arrived(1)

    pl.when(tm <= 1)(lambda: relay_halo(0))
    pl.when(tm == 0)(lambda: relay_halo(1))
    arrived(2)
    weights[6].wait()
    pl.when(tm <= 1)(cache_two.wait)
    pl.when(tm == 0)(cache_one.wait)
    from_halo(2)
    taps(2, True)
    if N > 2:
        pl.when(tm >= 2)(older)
    pl.when(tm >= 1)(lambda: forwarded(1, 0))
    from_halo(0)
    taps(0, False)
    pl.when(tm >= 1)(newer)
    from_halo(1)
    taps(1, False)

    there = jo.at[pl.ds(o * hr, hr)]
    send(jt, there, s_pair, r_pair, dev(core=o)).wait_recv()
    cell = lax.rem(lax.broadcasted_iota(jnp.int32, (T, S), 0), W)
    before = jnp.where(cell == 0, 0.0, parts[0, pl.ds(7, T)])
    after = jnp.where(cell == W - 1, 0.0, parts[2, pl.ds(9, T)])
    conv = before + parts[1, pl.ds(8, T)] + after
    out_ref[0] = (jo[...].reshape(T, S).astype(F32) + conv).astype(BF16).reshape(R, W, S)

    joined_copy.wait_send()
    for r in range(hr):
        pair(r).wait_send()
        pl.when(z < Z - 1)(rightward(z, r).wait_send)
        pl.when(z > 0)(leftward(z, r).wait_send)
        sideward(z, r).wait_send()

    def finish(d, carry):
        lo, hi = z - d, z + d

        for r in range(hr):

            @pl.when(lo >= 0)
            def _():
                pl.when(z < Z - 1)(rightward(lo, r).wait_send)
                sideward(lo, r).wait_send()

            @pl.when(hi < Z)
            def _():
                pl.when(z > 0)(leftward(hi, r).wait_send)
                sideward(hi, r).wait_send()

        return carry

    lax.fori_loop(1, Z, finish, 0)
    cache_edges(lambda copy: copy.wait_send())
    for f in range(3):
        both_sides(lambda side: halo_half(f, side, c).wait_send())
    for part in (0, 1):
        for hop in (1, 2):
            if N > hop:
                pl.when(tm + hop < N)(along_tm(hop, part).wait_send)

    def spread_done(f):
        edge_copy(f, 0).wait_send()
        rest_copy(f).wait_send()

        @pl.when(has_near)
        def _():
            edge_copy(f, 1).wait_send()
            edge_copy(f, 2).wait_send()

    spread_done(2)
    pl.when(tm >= 1)(lambda: spread_done(1))
    if N > 2:
        pl.when(tm >= 2)(lambda: spread_done(0))


def solution(mesh):
    Z, N = mesh.shape["space"], mesh.shape["tm"]

    def body(frames_in, cache, gain_one, gain_two, w_query, w_key, w_value, w_out, conv_weight):
        _, R, W, S = frames_in.shape
        C = 2 * S
        hr, half, T = R // 2, R // 2 * W, R * W
        dma = pltpu.SemaphoreType.DMA
        hbm = pl.BlockSpec(memory_space=pltpu.HBM)
        vmem = pl.BlockSpec(memory_space=pltpu.VMEM)
        return pl.pallas_call(
            functools.partial(kernel, Z, N),
            out_shape=jax.ShapeDtypeStruct(frames_in.shape, BF16),
            in_specs=[hbm] * 9,
            out_specs=vmem,
            scratch_shapes=[
                pltpu.VMEM((2, hr, W, S), BF16),
                pltpu.VMEM((Z, 2, hr, W, C), BF16),
                pltpu.VMEM((half, C), BF16),
                pltpu.VMEM((half, 1), F32),
                pltpu.VMEM((half, 1), F32),
                pltpu.VMEM((half, C), F32),
                pltpu.VMEM((3, R + 2, W, C), BF16),
                pltpu.VMEM((hr, W, S), BF16),
                pltpu.VMEM((R, W, S), BF16),
                pltpu.VMEM((3, T + 16, S), F32),
                pltpu.VMEM((C,), BF16),
                pltpu.VMEM((C,), BF16),
                pltpu.VMEM((C, C), BF16),
                pltpu.VMEM((C, C), BF16),
                pltpu.VMEM((C, C), BF16),
                pltpu.VMEM((C, C), BF16),
                pltpu.VMEM((3, 3, 3, S, C), BF16),
                dma((10,)),
                dma,
                dma,
                dma((hr,)),
                dma((hr,)),
                dma((Z, hr)),
                dma((Z, hr)),
                dma((Z, hr)),
                dma((Z, hr)),
                dma((Z, hr)),
                dma((2, 2)),
                dma((3, 2)),
                dma((3, 3)),
                dma((3,)),
                dma((3,)),
                dma((3,)),
                dma((2, 2)),
                dma((2, 2)),
                dma((3, 2)),
                dma((3, 2)),
            ],
            compiler_params=pltpu.CompilerParams(
                collective_id=0, has_side_effects=True, vmem_limit_bytes=50 << 20
            ),
        )(*(pltpu.with_memory_space_constraint(a, pltpu.HBM) for a in (
            frames_in, cache, gain_one, gain_two,
            w_query, w_key, w_value, w_out, jnp.swapaxes(conv_weight, 3, 4),
        )))

    return jax.shard_map(
        body,
        mesh=mesh,
        in_specs=(
            P(("clips", "tm"), "space", None, "chan"),
            P("clips", "space", None, None),
            P(),
            P(),
            P(),
            P(),
            P(),
            P(),
            P(None, None, None, None, "chan"),
        ),
        out_specs=P(("clips", "tm"), "space", None, "chan"),
        check_vma=False,
    )
```

```python
import functools
import math

import jax
import jax.numpy as jnp
from jax import lax
from jax.experimental import pallas as pl
from jax.experimental.pallas import tpu as pltpu
from jax.sharding import PartitionSpec as P

F32 = jnp.float32
BF16 = jnp.bfloat16
MESH = pl.DeviceIdType.MESH


def normalized(wide, gain):
    factor = lax.rsqrt(jnp.mean(wide * wide, axis=-1, keepdims=True) + 1e-06)
    return wide * factor * gain.astype(F32).reshape(1, -1)


def kernel(
    Z, N,
    x_hbm, cache_hbm, g1_hbm, g2_hbm, wq_hbm, wk_hbm, wv_hbm, wo_hbm, cw_hbm,
    out_ref,
    xr, xg, qk, top, total, acc, cb, jt, jo, parts, g1_ref, g2_ref, wq, wk, wv, wo, cw,
    s_loc, s_pair, r_pair, s_first, r_first, s_right, s_left, s_sib, r_z, r_sib,
    s_cache, r_halo, s_edge, s_rest, r_edge, r_rest, s_tm, r_tm, s_half, r_half,
):
    z = lax.axis_index("space")
    c = lax.axis_index("chan")
    tm = lax.axis_index("tm")
    o = 1 - c
    R, W, S = out_ref.shape[1:]
    C = 2 * S
    hr = R // 2
    half = hr * W
    T = R * W
    hw = W // 2

    def dev(dz=None, core=None, frame=None):
        return {
            "space": z if dz is None else dz,
            "chan": c if core is None else core,
            "tm": tm if frame is None else frame,
        }

    def send(src, dst, ssem, rsem, to):
        return pltpu.make_async_remote_copy(
            src_ref=src, dst_ref=dst, send_sem=ssem, recv_sem=rsem,
            device_id=to, device_id_type=MESH,
        )

    near = z + 2 * c - 1
    has_near = jnp.logical_and(near >= 0, near < Z)

    barrier = pltpu.get_barrier_semaphore()

    def greet(to):
        pl.semaphore_signal(barrier, inc=1, device_id=to, device_id_type=MESH)

    greet(dev(core=o))
    pl.when(z > 0)(lambda: greet(dev(dz=z - 1)))
    pl.when(z < Z - 1)(lambda: greet(dev(dz=z + 1)))
    pl.when(has_near)(lambda: greet(dev(dz=near, core=o)))
    for hop in (1, 2):
        if N > hop:
            pl.when(tm >= hop)(functools.partial(lambda h: greet(dev(frame=tm - h)), hop))

    x_own = pltpu.make_async_copy(x_hbm.at[0, pl.ds(c * hr, hr)], xr.at[c], s_loc.at[0])
    x_own.start()
    pieces = (
        (g1_hbm, g1_ref), (wq_hbm, wq), (wk_hbm, wk), (wv_hbm, wv), (wo_hbm, wo), (g2_hbm, g2_ref),
        (cw_hbm, cw),
    )
    weights = [
        pltpu.make_async_copy(a, b, s_loc.at[1 + i])
        for i, (a, b) in enumerate(pieces)
    ]
    for w in weights:
        w.start()
    first = jnp.minimum(tm, 1)
    cache_two = pltpu.make_async_copy(cache_hbm.at[first], cb.at[0, pl.ds(1, R)], s_loc.at[8])
    cache_one = pltpu.make_async_copy(cache_hbm.at[1], cb.at[1, pl.ds(1, R)], s_loc.at[9])
    pl.when(tm <= 1)(cache_two.start)
    pl.when(tm == 0)(cache_one.start)

    want = 1 + jnp.where(z > 0, 1, 0) + jnp.where(z < Z - 1, 1, 0) + jnp.where(has_near, 1, 0)
    for hop in (1, 2):
        if N > hop:
            want = want + jnp.where(tm + hop < N, 1, 0)
    pl.semaphore_wait(barrier, want)

    def pair(r):
        return send(x_hbm.at[0, o * hr + r], xr.at[c, r], s_first.at[r], r_first.at[r], dev(core=o))

    for r in range(hr):
        pair(r).start()

    blank = jnp.zeros((W, C), BF16)

    @pl.when(z == 0)
    def _():
        for f in range(3):
            cb[f, 0] = blank

    @pl.when(z == Z - 1)
    def _():
        for f in range(3):
            cb[f, R + 1] = blank

    x_own.wait()
    weights[0].wait()
    def tokens(row, count):
        at = pl.ds(row, count)
        return jnp.concatenate(
            [xr[k, at].reshape(count * W, S).astype(F32) for k in range(2)], axis=-1
        )

    def rightward(j, r):
        return send(xg.at[j, r, c], xg.at[j, r, c], s_right.at[j, r], r_z.at[j, r], dev(dz=z + 1))

    def leftward(j, r):
        return send(xg.at[j, r, c], xg.at[j, r, c], s_left.at[j, r], r_z.at[j, r], dev(dz=z - 1))

    def sideward(j, r):
        return send(xg.at[j, r, c], xg.at[j, r, c], s_sib.at[j, r], r_sib.at[j, r], dev(core=o))

    for r in range(hr):
        pair(r).wait_recv()
        normed = normalized(tokens(r, 1), g1_ref[...]).astype(BF16)
        xg[z, r, c] = normed.reshape(W, C)
        pl.when(z < Z - 1)(rightward(z, r).start)
        pl.when(z > 0)(leftward(z, r).start)
        sideward(z, r).start()

    for w in weights[1:3]:
        w.wait()
    query = jnp.dot(jnp.concatenate([xg[z, r, c] for r in range(hr)], axis=0), wq[...], preferred_element_type=F32).astype(BF16)
    folded = lax.dot_general(query, wk[...], (((1,), (1,)), ((), ())), preferred_element_type=F32)
    qk[...] = (folded * (C ** (-0.5) * math.log2(math.e))).astype(BF16)
    top[...] = jnp.full(top.shape, -1e30, F32)
    total[...] = jnp.zeros(total.shape, F32)
    acc[...] = jnp.zeros(acc.shape, F32)

    def attend(j, r):
        keys = xg[j, r].reshape(2 * W, C)
        scores = lax.dot_general(qk[...], keys, (((1,), (1,)), ((), ())), preferred_element_type=F32)
        old = top[...]
        new = jnp.maximum(old, jnp.max(scores, axis=-1, keepdims=True))
        weight = jnp.exp2(scores - new)
        fade = jnp.exp2(old - new)
        top[...] = new
        total[...] = total[...] * fade + jnp.sum(weight, axis=-1, keepdims=True)
        acc[...] = acc[...] * fade + jnp.dot(weight.astype(BF16), keys, preferred_element_type=F32)

    for r in range(hr):
        sideward(z, r).wait_recv()
        attend(z, r)

    def cache_edge(f, side):
        row = R - 1 if side == 0 else 0
        cells = pl.ds(pl.multiple_of(c * hw, hw), hw)
        source = cache_hbm.at[first if f == 0 else 1, row, cells]
        to = dev(dz=z + 1) if side == 0 else dev(dz=z - 1)
        return send(source, cb.at[f, 0 if side == 0 else R + 1, cells], s_cache.at[f, side], r_halo.at[f, side], to)

    def cache_edges(act):
        for side, there in ((0, z < Z - 1), (1, z > 0)):
            pl.when(jnp.logical_and(there, tm <= 1))(lambda s=side: act(cache_edge(0, s)))
            pl.when(jnp.logical_and(there, tm == 0))(lambda s=side: act(cache_edge(1, s)))

    def step(d, carry):
        lo, hi = z - d, z + d
        has_lo, has_hi = lo >= 0, hi < Z

        for r in range(hr):

            @pl.when(has_lo)
            def _():
                rightward(lo, r).wait_recv()
                pl.when(z < Z - 1)(rightward(lo, r).start)
                sideward(lo, r).start()

            @pl.when(has_hi)
            def _():
                leftward(hi, r).wait_recv()
                pl.when(z > 0)(leftward(hi, r).start)
                sideward(hi, r).start()

            if r == hr - 1:
                pl.when(d == Z - 1)(lambda: cache_edges(lambda copy: copy.start()))

            @pl.when(has_lo)
            def _():
                sideward(lo, r).wait_recv()
                attend(lo, r)

            @pl.when(has_hi)
            def _():
                sideward(hi, r).wait_recv()
                attend(hi, r)

        return carry

    lax.fori_loop(1, Z, step, 0)

    for w in weights[3:6]:
        w.wait()
    def finish_rows(row, count):
        at = pl.ds(pl.multiple_of(row * W, W), count * W)
        mixed = (acc[at, :] * (1.0 / total[at, :])).astype(BF16)
        attended = jnp.dot(mixed, wv[...], preferred_element_type=F32).astype(BF16)
        joined = tokens(row, count) + jnp.dot(attended, wo[...], preferred_element_type=F32)
        joined = joined.astype(BF16).astype(F32)
        scaled = normalized(joined, g2_ref[...])
        act = (scaled / (1.0 + jnp.exp(-scaled))).astype(BF16)
        cb[2, pl.ds(1 + c * hr + row, count)] = act.reshape(count, W, C)
        low, high = joined[:, :S].astype(BF16), joined[:, S:].astype(BF16)
        jo[pl.ds(c * hr + row, count)] = jnp.where(c == 0, low, high).reshape(count, W, S)
        jt[pl.ds(row, count)] = jnp.where(c == 0, high, low).reshape(count, W, S)

    edge = jnp.where(c == 0, 1, R)
    rest = jnp.where(c == 0, 2, 1 + hr)
    far = jnp.where(c == 0, R + 1, 0)

    def along_tm(hop, part):
        row = cb.at[2, edge] if part == 0 else cb.at[2, pl.ds(rest, hr - 1)]
        there = cb.at[2 - hop, edge] if part == 0 else cb.at[2 - hop, pl.ds(rest, hr - 1)]
        return send(row, there, s_tm.at[hop - 1, part], r_tm.at[hop - 1, part], dev(frame=tm + hop))

    def edge_copy(f, k):
        src = cb.at[f, edge]
        if k == 0:
            return send(src, src, s_edge.at[f, 0], r_edge.at[f], dev(core=o))
        cells = pl.ds((k - 1) * hw, hw)
        return send(
            cb.at[f, edge, cells], cb.at[f, far, cells], s_edge.at[f, k], r_halo.at[f, o],
            dev(dz=near, core=k - 1),
        )

    def rest_copy(f):
        src = cb.at[f, pl.ds(rest, hr - 1)]
        return send(src, src, s_rest.at[f], r_rest.at[f], dev(core=o))

    def from_sibling(f):
        there = jnp.where(c == 0, R, 1)
        others = jnp.where(c == 0, 1 + hr, 2)
        row = cb.at[f, there]
        send(row, row, s_edge.at[f, 0], r_edge.at[f], dev(core=o)).wait_recv()
        rows = cb.at[f, pl.ds(others, hr - 1)]
        send(rows, rows, s_rest.at[f], r_rest.at[f], dev(core=o)).wait_recv()

    def halo_half(f, side, core):
        half_row = cb.at[f, 0 if side == 0 else R + 1, pl.ds(pl.multiple_of(core * hw, hw), hw)]
        return send(half_row, half_row, s_half.at[f, side], r_half.at[f, side], dev(core=o))

    def both_sides(visit):
        pl.when(z > 0)(lambda: visit(0))
        pl.when(z < Z - 1)(lambda: visit(1))

    def relay_halo(f):
        def visit(side):
            half_row = cb.at[f, 0 if side == 0 else R + 1, pl.ds(pl.multiple_of(c * hw, hw), hw)]
            send(half_row, half_row, s_edge.at[f, 1], r_halo.at[f, side], dev(core=o)).wait_recv()
            halo_half(f, side, c).start()

        both_sides(visit)

    def from_halo(f):
        both_sides(lambda side: halo_half(f, side, o).wait_recv())

    def spread_edge(f):
        edge_copy(f, 0).start()

        @pl.when(has_near)
        def _():
            edge_copy(f, 1).start()
            edge_copy(f, 2).start()

    for part in (0, 1):
        if part == 0:
            finish_rows(edge - 1 - c * hr, 1)
        else:
            finish_rows(rest - 1 - c * hr, hr - 1)
        for hop in (1, 2):
            if N > hop:
                pl.when(tm + hop < N)(along_tm(hop, part).start)
        if part == 0:
            spread_edge(2)
        else:
            rest_copy(2).start()

    joined_copy = send(jt, jo.at[pl.ds(c * hr, hr)], s_pair, r_pair, dev(core=o))
    joined_copy.start()

    def taps(f, start):
        rows = jnp.concatenate([cb[f, dh : dh + R].reshape(T, C) for dh in range(3)], axis=-1)
        for dw in range(3):
            kernel_rows = jnp.concatenate([cw[f, dh, dw] for dh in range(3)], axis=-1)
            value = lax.dot_general(
                rows, kernel_rows, (((1,), (1,)), ((), ())), preferred_element_type=F32
            )
            if start:
                parts[dw, pl.ds(8, T)] = value
            else:
                parts[dw, pl.ds(8, T)] += value

    def forwarded(f, part):
        along_tm(2 - f, part).wait_recv()
        if part == 0:
            spread_edge(f)
        else:
            rest_copy(f).start()

    def arrived(f):
        relay_halo(f)
        from_sibling(f)

    def older():
        forwarded(0, 0)
        forwarded(0, 1)
        arrived(0)

    def newer():
        forwarded(1, 1)
        arrived(1)

    pl.when(tm <= 1)(lambda: relay_halo(0))
    pl.when(tm == 0)(lambda: relay_halo(1))
    arrived(2)
    weights[6].wait()
    pl.when(tm <= 1)(cache_two.wait)
    pl.when(tm == 0)(cache_one.wait)
    from_halo(2)
    taps(2, True)
    if N > 2:
        pl.when(tm >= 2)(older)
    pl.when(tm >= 1)(lambda: forwarded(1, 0))
    from_halo(0)
    taps(0, False)
    pl.when(tm >= 1)(newer)
    from_halo(1)
    taps(1, False)

    there = jo.at[pl.ds(o * hr, hr)]
    send(jt, there, s_pair, r_pair, dev(core=o)).wait_recv()
    cell = lax.rem(lax.broadcasted_iota(jnp.int32, (T, S), 0), W)
    before = jnp.where(cell == 0, 0.0, parts[0, pl.ds(7, T)])
    after = jnp.where(cell == W - 1, 0.0, parts[2, pl.ds(9, T)])
    conv = before + parts[1, pl.ds(8, T)] + after
    out_ref[0] = (jo[...].reshape(T, S).astype(F32) + conv).astype(BF16).reshape(R, W, S)

    joined_copy.wait_send()
    for r in range(hr):
        pair(r).wait_send()
        pl.when(z < Z - 1)(rightward(z, r).wait_send)
        pl.when(z > 0)(leftward(z, r).wait_send)
        sideward(z, r).wait_send()

    def finish(d, carry):
        lo, hi = z - d, z + d

        for r in range(hr):

            @pl.when(lo >= 0)
            def _():
                pl.when(z < Z - 1)(rightward(lo, r).wait_send)
                sideward(lo, r).wait_send()

            @pl.when(hi < Z)
            def _():
                pl.when(z > 0)(leftward(hi, r).wait_send)
                sideward(hi, r).wait_send()

        return carry

    lax.fori_loop(1, Z, finish, 0)
    cache_edges(lambda copy: copy.wait_send())
    for f in range(3):
        both_sides(lambda side: halo_half(f, side, c).wait_send())
    for part in (0, 1):
        for hop in (1, 2):
            if N > hop:
                pl.when(tm + hop < N)(along_tm(hop, part).wait_send)

    def spread_done(f):
        edge_copy(f, 0).wait_send()
        rest_copy(f).wait_send()

        @pl.when(has_near)
        def _():
            edge_copy(f, 1).wait_send()
            edge_copy(f, 2).wait_send()

    spread_done(2)
    pl.when(tm >= 1)(lambda: spread_done(1))
    if N > 2:
        pl.when(tm >= 2)(lambda: spread_done(0))


def solution(mesh):
    Z, N = mesh.shape["space"], mesh.shape["tm"]

    def body(frames_in, cache, gain_one, gain_two, w_query, w_key, w_value, w_out, conv_weight):
        _, R, W, S = frames_in.shape
        C = 2 * S
        hr, half, T = R // 2, R // 2 * W, R * W
        dma = pltpu.SemaphoreType.DMA
        hbm = pl.BlockSpec(memory_space=pltpu.HBM)
        vmem = pl.BlockSpec(memory_space=pltpu.VMEM)
        return pl.pallas_call(
            functools.partial(kernel, Z, N),
            out_shape=jax.ShapeDtypeStruct(frames_in.shape, BF16),
            in_specs=[hbm] * 9,
            out_specs=vmem,
            scratch_shapes=[
                pltpu.VMEM((2, hr, W, S), BF16),
                pltpu.VMEM((Z, hr, 2, W, C), BF16),
                pltpu.VMEM((half, C), BF16),
                pltpu.VMEM((half, 1), F32),
                pltpu.VMEM((half, 1), F32),
                pltpu.VMEM((half, C), F32),
                pltpu.VMEM((3, R + 2, W, C), BF16),
                pltpu.VMEM((hr, W, S), BF16),
                pltpu.VMEM((R, W, S), BF16),
                pltpu.VMEM((3, T + 16, S), F32),
                pltpu.VMEM((C,), BF16),
                pltpu.VMEM((C,), BF16),
                pltpu.VMEM((C, C), BF16),
                pltpu.VMEM((C, C), BF16),
                pltpu.VMEM((C, C), BF16),
                pltpu.VMEM((C, C), BF16),
                pltpu.VMEM((3, 3, 3, S, C), BF16),
                dma((10,)),
                dma,
                dma,
                dma((hr,)),
                dma((hr,)),
                dma((Z, hr)),
                dma((Z, hr)),
                dma((Z, hr)),
                dma((Z, hr)),
                dma((Z, hr)),
                dma((2, 2)),
                dma((3, 2)),
                dma((3, 3)),
                dma((3,)),
                dma((3,)),
                dma((3,)),
                dma((2, 2)),
                dma((2, 2)),
                dma((3, 2)),
                dma((3, 2)),
            ],
            compiler_params=pltpu.CompilerParams(
                collective_id=0, has_side_effects=True, vmem_limit_bytes=50 << 20
            ),
        )(*(pltpu.with_memory_space_constraint(a, pltpu.HBM) for a in (
            frames_in, cache, gain_one, gain_two,
            w_query, w_key, w_value, w_out, jnp.swapaxes(conv_weight, 3, 4),
        )))

    return jax.shard_map(
        body,
        mesh=mesh,
        in_specs=(
            P(("clips", "tm"), "space", None, "chan"),
            P("clips", "space", None, None),
            P(),
            P(),
            P(),
            P(),
            P(),
            P(),
            P(None, None, None, None, "chan"),
        ),
        out_specs=P(("clips", "tm"), "space", None, "chan"),
        check_vma=False,
    )
```

```python
import functools
import math

import jax
import jax.numpy as jnp
from jax import lax
from jax.experimental import pallas as pl
from jax.experimental.pallas import tpu as pltpu
from jax.sharding import PartitionSpec as P

F32 = jnp.float32
BF16 = jnp.bfloat16
MESH = pl.DeviceIdType.MESH


def normalized(wide, gain):
    factor = lax.rsqrt(jnp.mean(wide * wide, axis=-1, keepdims=True) + 1e-06)
    return wide * factor * gain.astype(F32).reshape(1, -1)


def kernel(
    Z, N,
    x_hbm, cache_hbm, g1_hbm, g2_hbm, wq_hbm, wk_hbm, wv_hbm, wo_hbm, cw_hbm,
    out_ref,
    xr, xg, qk, top, total, acc, cb, jt, jo, parts, g1_ref, g2_ref, wq, wk, wv, wo, cw,
    s_loc, s_pair, r_pair, s_first, r_first, s_right, s_left, s_sib, r_z, r_sib,
    s_cache, r_halo, s_edge, s_rest, r_edge, r_rest, s_tm, r_tm, s_half, r_half,
):
    z = lax.axis_index("space")
    c = lax.axis_index("chan")
    tm = lax.axis_index("tm")
    o = 1 - c
    R, W, S = out_ref.shape[1:]
    C = 2 * S
    hr = R // 2
    half = hr * W
    T = R * W
    hw = W // 2

    def dev(dz=None, core=None, frame=None):
        return {
            "space": z if dz is None else dz,
            "chan": c if core is None else core,
            "tm": tm if frame is None else frame,
        }

    def send(src, dst, ssem, rsem, to):
        return pltpu.make_async_remote_copy(
            src_ref=src, dst_ref=dst, send_sem=ssem, recv_sem=rsem,
            device_id=to, device_id_type=MESH,
        )

    near = z + 2 * c - 1
    has_near = jnp.logical_and(near >= 0, near < Z)

    barrier = pltpu.get_barrier_semaphore()

    def greet(to):
        pl.semaphore_signal(barrier, inc=1, device_id=to, device_id_type=MESH)

    greet(dev(core=o))
    pl.when(z > 0)(lambda: greet(dev(dz=z - 1)))
    pl.when(z < Z - 1)(lambda: greet(dev(dz=z + 1)))
    pl.when(has_near)(lambda: greet(dev(dz=near, core=o)))
    for hop in (1, 2):
        if N > hop:
            pl.when(tm >= hop)(functools.partial(lambda h: greet(dev(frame=tm - h)), hop))

    x_own = pltpu.make_async_copy(x_hbm.at[0, pl.ds(c * hr, hr)], xr.at[c], s_loc.at[0])
    x_own.start()
    pieces = (
        (g1_hbm, g1_ref), (wq_hbm, wq), (wk_hbm, wk), (wv_hbm, wv), (wo_hbm, wo), (g2_hbm, g2_ref),
        (cw_hbm, cw),
    )
    weights = [
        pltpu.make_async_copy(a, b, s_loc.at[1 + i])
        for i, (a, b) in enumerate(pieces)
    ]
    for w in weights:
        w.start()
    first = jnp.minimum(tm, 1)
    cache_two = pltpu.make_async_copy(cache_hbm.at[first], cb.at[0, pl.ds(1, R)], s_loc.at[8])
    cache_one = pltpu.make_async_copy(cache_hbm.at[1], cb.at[1, pl.ds(1, R)], s_loc.at[9])
    pl.when(tm <= 1)(cache_two.start)
    pl.when(tm == 0)(cache_one.start)

    want = 1 + jnp.where(z > 0, 1, 0) + jnp.where(z < Z - 1, 1, 0) + jnp.where(has_near, 1, 0)
    for hop in (1, 2):
        if N > hop:
            want = want + jnp.where(tm + hop < N, 1, 0)
    pl.semaphore_wait(barrier, want)

    def pair(r):
        return send(x_hbm.at[0, o * hr + r], xr.at[c, r], s_first.at[r], r_first.at[r], dev(core=o))

    for r in range(hr):
        pair(r).start()

    blank = jnp.zeros((W, C), BF16)

    @pl.when(z == 0)
    def _():
        for f in range(3):
            cb[f, 0] = blank

    @pl.when(z == Z - 1)
    def _():
        for f in range(3):
            cb[f, R + 1] = blank

    x_own.wait()
    weights[0].wait()
    def tokens(row, count):
        at = pl.ds(row, count)
        return jnp.concatenate(
            [xr[k, at].reshape(count * W, S).astype(F32) for k in range(2)], axis=-1
        )

    def rightward(j, r):
        return send(xg.at[j, r, c], xg.at[j, r, c], s_right.at[j, r], r_z.at[j, r], dev(dz=z + 1))

    def leftward(j, r):
        return send(xg.at[j, r, c], xg.at[j, r, c], s_left.at[j, r], r_z.at[j, r], dev(dz=z - 1))

    def sideward(j, r):
        return send(xg.at[j, r, c], xg.at[j, r, c], s_sib.at[j, r], r_sib.at[j, r], dev(core=o))

    for r in range(hr):
        pair(r).wait_recv()
        normed = normalized(tokens(r, 1), g1_ref[...]).astype(BF16)
        xg[z, r, c] = normed.reshape(W, C)
        pl.when(z < Z - 1)(rightward(z, r).start)
        pl.when(z > 0)(leftward(z, r).start)
        sideward(z, r).start()

    for w in weights[1:3]:
        w.wait()
    query = jnp.dot(jnp.concatenate([xg[z, r, c] for r in range(hr)], axis=0), wq[...], preferred_element_type=F32).astype(BF16)
    folded = lax.dot_general(query, wk[...], (((1,), (1,)), ((), ())), preferred_element_type=F32)
    qk[...] = (folded * (C ** (-0.5) * math.log2(math.e))).astype(BF16)
    top[...] = jnp.full(top.shape, -1e30, F32)
    total[...] = jnp.zeros(total.shape, F32)
    acc[...] = jnp.zeros(acc.shape, F32)

    def attend(j, r):
        keys = xg[j, r].reshape(2 * W, C)
        scores = lax.dot_general(qk[...], keys, (((1,), (1,)), ((), ())), preferred_element_type=F32)
        old = top[...]
        new = jnp.maximum(old, jnp.max(scores, axis=-1, keepdims=True))
        weight = jnp.exp2(scores - new)
        fade = jnp.exp2(old - new)
        top[...] = new
        total[...] = total[...] * fade + jnp.sum(weight, axis=-1, keepdims=True)
        acc[...] = acc[...] * fade + jnp.dot(weight.astype(BF16), keys, preferred_element_type=F32)

    for r in range(hr):
        sideward(z, r).wait_recv()
        attend(z, r)

    def cache_edge(f, side):
        row = R - 1 if side == 0 else 0
        cells = pl.ds(pl.multiple_of(c * hw, hw), hw)
        source = cache_hbm.at[first if f == 0 else 1, row, cells]
        to = dev(dz=z + 1) if side == 0 else dev(dz=z - 1)
        return send(source, cb.at[f, 0 if side == 0 else R + 1, cells], s_cache.at[f, side], r_halo.at[f, side], to)

    def cache_edges(act):
        for side, there in ((0, z < Z - 1), (1, z > 0)):
            pl.when(jnp.logical_and(there, tm <= 1))(lambda s=side: act(cache_edge(0, s)))
            pl.when(jnp.logical_and(there, tm == 0))(lambda s=side: act(cache_edge(1, s)))

    def step(d, carry):
        lo, hi = z - d, z + d
        has_lo, has_hi = lo >= 0, hi < Z

        for r in range(hr):

            @pl.when(has_lo)
            def _():
                rightward(lo, r).wait_recv()
                pl.when(z < Z - 1)(rightward(lo, r).start)
                sideward(lo, r).start()

            @pl.when(has_hi)
            def _():
                leftward(hi, r).wait_recv()
                pl.when(z > 0)(leftward(hi, r).start)
                sideward(hi, r).start()

            if r == hr - 1:
                pl.when(d == Z - 1)(lambda: cache_edges(lambda copy: copy.start()))

            @pl.when(has_lo)
            def _():
                sideward(lo, r).wait_recv()
                attend(lo, r)

            @pl.when(has_hi)
            def _():
                sideward(hi, r).wait_recv()
                attend(hi, r)

        return carry

    lax.fori_loop(1, Z, step, 0)

    for w in weights[3:6]:
        w.wait()
    def finish_rows(row, count):
        at = pl.ds(pl.multiple_of(row * W, W), count * W)
        mixed = (acc[at, :] * (1.0 / total[at, :])).astype(BF16)
        attended = jnp.dot(mixed, wv[...], preferred_element_type=F32).astype(BF16)
        joined = tokens(row, count) + jnp.dot(attended, wo[...], preferred_element_type=F32)
        joined = joined.astype(BF16).astype(F32)
        scaled = normalized(joined, g2_ref[...])
        act = (scaled / (1.0 + jnp.exp(-scaled))).astype(BF16)
        cb[2, pl.ds(1 + c * hr + row, count)] = act.reshape(count, W, C)
        low, high = joined[:, :S].astype(BF16), joined[:, S:].astype(BF16)
        jo[pl.ds(c * hr + row, count)] = jnp.where(c == 0, low, high).reshape(count, W, S)
        jt[pl.ds(row, count)] = jnp.where(c == 0, high, low).reshape(count, W, S)

    edge = jnp.where(c == 0, 1, R)
    rest = jnp.where(c == 0, 2, 1 + hr)
    far = jnp.where(c == 0, R + 1, 0)

    def along_tm(hop, part):
        row = cb.at[2, edge] if part == 0 else cb.at[2, pl.ds(rest, hr - 1)]
        there = cb.at[2 - hop, edge] if part == 0 else cb.at[2 - hop, pl.ds(rest, hr - 1)]
        return send(row, there, s_tm.at[hop - 1, part], r_tm.at[hop - 1, part], dev(frame=tm + hop))

    def edge_copy(f, k):
        src = cb.at[f, edge]
        if k == 0:
            return send(src, src, s_edge.at[f, 0], r_edge.at[f], dev(core=o))
        cells = pl.ds((k - 1) * hw, hw)
        return send(
            cb.at[f, edge, cells], cb.at[f, far, cells], s_edge.at[f, k], r_halo.at[f, o],
            dev(dz=near, core=k - 1),
        )

    def rest_copy(f):
        src = cb.at[f, pl.ds(rest, hr - 1)]
        return send(src, src, s_rest.at[f], r_rest.at[f], dev(core=o))

    def from_sibling(f):
        there = jnp.where(c == 0, R, 1)
        others = jnp.where(c == 0, 1 + hr, 2)
        row = cb.at[f, there]
        send(row, row, s_edge.at[f, 0], r_edge.at[f], dev(core=o)).wait_recv()
        rows = cb.at[f, pl.ds(others, hr - 1)]
        send(rows, rows, s_rest.at[f], r_rest.at[f], dev(core=o)).wait_recv()

    def halo_half(f, side, core):
        half_row = cb.at[f, 0 if side == 0 else R + 1, pl.ds(pl.multiple_of(core * hw, hw), hw)]
        return send(half_row, half_row, s_half.at[f, side], r_half.at[f, side], dev(core=o))

    def both_sides(visit):
        pl.when(z > 0)(lambda: visit(0))
        pl.when(z < Z - 1)(lambda: visit(1))

    def relay_halo(f):
        def visit(side):
            half_row = cb.at[f, 0 if side == 0 else R + 1, pl.ds(pl.multiple_of(c * hw, hw), hw)]
            send(half_row, half_row, s_edge.at[f, 1], r_halo.at[f, side], dev(core=o)).wait_recv()
            halo_half(f, side, c).start()

        both_sides(visit)

    def from_halo(f):
        both_sides(lambda side: halo_half(f, side, o).wait_recv())

    def spread_edge(f):
        edge_copy(f, 0).start()

        @pl.when(has_near)
        def _():
            edge_copy(f, 1).start()
            edge_copy(f, 2).start()

    for part in (0, 1):
        if part == 0:
            finish_rows(edge - 1 - c * hr, 1)
        else:
            finish_rows(rest - 1 - c * hr, hr - 1)
        for hop in (1, 2):
            if N > hop:
                pl.when(tm + hop < N)(along_tm(hop, part).start)
        if part == 0:
            spread_edge(2)
        else:
            rest_copy(2).start()

    joined_copy = send(jt, jo.at[pl.ds(c * hr, hr)], s_pair, r_pair, dev(core=o))
    joined_copy.start()

    def taps(f, start):
        rows = jnp.concatenate([cb[f, dh : dh + R].reshape(T, C) for dh in range(3)], axis=-1)
        for dw in range(3):
            kernel_rows = jnp.concatenate([cw[f, dh, dw] for dh in range(3)], axis=-1)
            value = lax.dot_general(
                rows, kernel_rows, (((1,), (1,)), ((), ())), preferred_element_type=F32
            )
            if start:
                parts[dw, pl.ds(8, T)] = value
            else:
                parts[dw, pl.ds(8, T)] += value

    def forwarded(f, part):
        along_tm(2 - f, part).wait_recv()
        if part == 0:
            spread_edge(f)
        else:
            rest_copy(f).start()

    def arrived(f):
        relay_halo(f)
        from_sibling(f)

    def older():
        forwarded(0, 0)
        forwarded(0, 1)
        arrived(0)

    def newer():
        forwarded(1, 1)
        arrived(1)

    pl.when(tm <= 1)(lambda: relay_halo(0))
    pl.when(tm == 0)(lambda: relay_halo(1))
    inner = jnp.logical_and(z > 0, z < Z - 1)
    outer = jnp.logical_or(z == 0, z == Z - 1)
    pl.when(jnp.logical_and(tm >= 1, inner))(lambda: forwarded(1, 0))
    arrived(2)
    weights[6].wait()
    pl.when(tm <= 1)(cache_two.wait)
    pl.when(tm == 0)(cache_one.wait)
    from_halo(2)
    taps(2, True)
    if N > 2:
        pl.when(tm >= 2)(older)
    pl.when(jnp.logical_and(tm >= 1, outer))(lambda: forwarded(1, 0))
    from_halo(0)
    taps(0, False)
    pl.when(tm >= 1)(newer)
    from_halo(1)
    taps(1, False)

    there = jo.at[pl.ds(o * hr, hr)]
    send(jt, there, s_pair, r_pair, dev(core=o)).wait_recv()
    cell = lax.rem(lax.broadcasted_iota(jnp.int32, (T, S), 0), W)
    before = jnp.where(cell == 0, 0.0, parts[0, pl.ds(7, T)])
    after = jnp.where(cell == W - 1, 0.0, parts[2, pl.ds(9, T)])
    conv = before + parts[1, pl.ds(8, T)] + after
    out_ref[0] = (jo[...].reshape(T, S).astype(F32) + conv).astype(BF16).reshape(R, W, S)

    joined_copy.wait_send()
    for r in range(hr):
        pair(r).wait_send()
        pl.when(z < Z - 1)(rightward(z, r).wait_send)
        pl.when(z > 0)(leftward(z, r).wait_send)
        sideward(z, r).wait_send()

    def finish(d, carry):
        lo, hi = z - d, z + d

        for r in range(hr):

            @pl.when(lo >= 0)
            def _():
                pl.when(z < Z - 1)(rightward(lo, r).wait_send)
                sideward(lo, r).wait_send()

            @pl.when(hi < Z)
            def _():
                pl.when(z > 0)(leftward(hi, r).wait_send)
                sideward(hi, r).wait_send()

        return carry

    lax.fori_loop(1, Z, finish, 0)
    cache_edges(lambda copy: copy.wait_send())
    for f in range(3):
        both_sides(lambda side: halo_half(f, side, c).wait_send())
    for part in (0, 1):
        for hop in (1, 2):
            if N > hop:
                pl.when(tm + hop < N)(along_tm(hop, part).wait_send)

    def spread_done(f):
        edge_copy(f, 0).wait_send()
        rest_copy(f).wait_send()

        @pl.when(has_near)
        def _():
            edge_copy(f, 1).wait_send()
            edge_copy(f, 2).wait_send()

    spread_done(2)
    pl.when(tm >= 1)(lambda: spread_done(1))
    if N > 2:
        pl.when(tm >= 2)(lambda: spread_done(0))


def solution(mesh):
    Z, N = mesh.shape["space"], mesh.shape["tm"]

    def body(frames_in, cache, gain_one, gain_two, w_query, w_key, w_value, w_out, conv_weight):
        _, R, W, S = frames_in.shape
        C = 2 * S
        hr, half, T = R // 2, R // 2 * W, R * W
        dma = pltpu.SemaphoreType.DMA
        hbm = pl.BlockSpec(memory_space=pltpu.HBM)
        vmem = pl.BlockSpec(memory_space=pltpu.VMEM)
        return pl.pallas_call(
            functools.partial(kernel, Z, N),
            out_shape=jax.ShapeDtypeStruct(frames_in.shape, BF16),
            in_specs=[hbm] * 9,
            out_specs=vmem,
            scratch_shapes=[
                pltpu.VMEM((2, hr, W, S), BF16),
                pltpu.VMEM((Z, hr, 2, W, C), BF16),
                pltpu.VMEM((half, C), BF16),
                pltpu.VMEM((half, 1), F32),
                pltpu.VMEM((half, 1), F32),
                pltpu.VMEM((half, C), F32),
                pltpu.VMEM((3, R + 2, W, C), BF16),
                pltpu.VMEM((hr, W, S), BF16),
                pltpu.VMEM((R, W, S), BF16),
                pltpu.VMEM((3, T + 16, S), F32),
                pltpu.VMEM((C,), BF16),
                pltpu.VMEM((C,), BF16),
                pltpu.VMEM((C, C), BF16),
                pltpu.VMEM((C, C), BF16),
                pltpu.VMEM((C, C), BF16),
                pltpu.VMEM((C, C), BF16),
                pltpu.VMEM((3, 3, 3, S, C), BF16),
                dma((10,)),
                dma,
                dma,
                dma((hr,)),
                dma((hr,)),
                dma((Z, hr)),
                dma((Z, hr)),
                dma((Z, hr)),
                dma((Z, hr)),
                dma((Z, hr)),
                dma((2, 2)),
                dma((3, 2)),
                dma((3, 3)),
                dma((3,)),
                dma((3,)),
                dma((3,)),
                dma((2, 2)),
                dma((2, 2)),
                dma((3, 2)),
                dma((3, 2)),
            ],
            compiler_params=pltpu.CompilerParams(
                collective_id=0, has_side_effects=True, vmem_limit_bytes=50 << 20
            ),
        )(*(pltpu.with_memory_space_constraint(a, pltpu.HBM) for a in (
            frames_in, cache, gain_one, gain_two,
            w_query, w_key, w_value, w_out, jnp.swapaxes(conv_weight, 3, 4),
        )))

    return jax.shard_map(
        body,
        mesh=mesh,
        in_specs=(
            P(("clips", "tm"), "space", None, "chan"),
            P("clips", "space", None, None),
            P(),
            P(),
            P(),
            P(),
            P(),
            P(),
            P(None, None, None, None, "chan"),
        ),
        out_specs=P(("clips", "tm"), "space", None, "chan"),
        check_vma=False,
    )
```
